32 devices in a mesh: freq: 8 (over y, x, core), tile: 4 (over z).
Axes of the slice: x: 2, y: 2, z: 4, core: 2. Of those that a mesh axis runs over, the one named last changes fastest.
Arguments:
- left_factor: bfloat16 [128, 8, 32, 2, 16, 256], P('freq', 'tile'), may hold values from -1.5 to 1.5
- right_factor: bfloat16 [128, 8, 32, 2, 16, 256], P('freq', None, 'tile'), may hold values from -0.0625 to 0.0625
- tile_ranks: int32 [128, 8, 32], P('freq'), may hold values from 1 to 16
- tile_scales: float32 [128, 2, 8, 32], P('freq'), may hold values from 0.5 to 2
- recorded: float32 [128, 2, 8, 2048], P('freq', None, None, 'tile'), may hold values from -12 to 12
- step_sizes: float32 [128], P('freq'), may hold values from 0.2 to 0.6
- thresholds: float32 [8], replicated, may hold values from 0.1 to 0.5
Outputs:
- estimate: float32 [128, 2, 8, 8192], P('freq', None, None, 'tile')
The draws below stay inside these ranges and needn't reach their ends.
Inputs may be any that keep to these rules, and one draw needn't show every extreme that they name: `tile_ranks`: rank of each tile; rank slots at and above it carry no weight.
All inputs are finite; a program needn't handle non-finite values.
Results may differ from the reference program's by a relative error of at most 0.0058.
Values may be sent and summed in bfloat16 or wider, within the bound.
A program may use at most 128 MiB of HBM per device.

```python
import math
import jax
import jax.numpy as jnp
from jax import lax

TS = 256
R = 16
NV = 8
F = 128
NCT = 32
NRT = 8
NR = 2048
NC = 8192


def plant(entries, key, smallest, largest):
    longest = entries.shape.index(max(entries.shape))
    spots = []
    for shift in (0, 1):
        where = [jax.random.randint(jax.random.fold_in(key, axis), (), 0, length) for axis, length in enumerate(entries.shape)]
        where[longest] = (where[longest] + shift) % entries.shape[longest]
        spots.append(tuple(where))
    return entries.at[spots[0]].set(smallest).at[spots[1]].set(largest)


def steps_of(own_key, dims, split, low, largest):
    level = 1.0
    for axis_at, blocks in split:
        draws = jax.random.uniform(jax.random.fold_in(jax.random.fold_in(own_key, 6), axis_at), (blocks,), jnp.float32, low / len(split), largest / len(split))
        level = level * jnp.repeat(jnp.exp(draws), dims[axis_at] // blocks).reshape((-1,) + (1,) * (len(dims) - 1 - axis_at))
    return level


def normal_values(key, shape, deviation, bound, cuts=(), kind=jnp.bfloat16):
    result = deviation * jax.random.normal(key, shape, jnp.float32)
    if cuts:
        result = result * steps_of(key, shape, cuts, -0.22, 0.18)
    return jnp.clip(result, -bound, bound).astype(kind)


def setup_inputs(seed: int = 0) -> dict:
    keys = jax.random.split(jax.random.key(seed), 8)
    return {
        "left_factor": normal_values(keys[0], (F, NRT, NCT, 2, R, TS), R ** -0.5, 1.5, ((0, 8), (1, 4))),
        "right_factor": normal_values(keys[1], (F, NRT, NCT, 2, R, TS), NC ** -0.5, 0.0625, ((0, 8), (2, 4))),
        "tile_ranks": plant(jax.random.randint(keys[2], (F, NRT, NCT), 1, R + 1), jax.random.fold_in(keys[2], 1), 1, R).astype(jnp.int32),
        "tile_scales": jnp.clip(jnp.exp(math.log(2.0) - 1.3862944 * jax.random.uniform(keys[3], (F, 2, NRT, NCT), jnp.float32) ** steps_of(keys[3], (F, 2, NRT, NCT), ((0, 8),), -0.2, 0.2)), 0.5, 2.0),
        "recorded": normal_values(keys[4], (F, 2, NV, NR), 2.0, 12.0, ((0, 8), (3, 4)), jnp.float32),
        "step_sizes": jnp.clip(jnp.exp(math.log(0.6) - 1.0986123 * jax.random.uniform(keys[5], (F,), jnp.float32) ** steps_of(keys[5], (F,), ((0, 8),), -0.2, 0.2)), 0.2, 0.6),
        "thresholds": jnp.clip(jnp.exp(jax.random.uniform(keys[6], (NV,), jnp.float32, math.log(0.1), math.log(0.5))), 0.1, 0.5),
    }


def dft_tables(freq_index, time_count):
    times_row = jnp.arange(time_count, dtype=jnp.int32)
    phase_steps = (freq_index[:, None] * times_row[None, :] % time_count).astype(jnp.float32)
    angles = phase_steps * (2.0 * math.pi / time_count)
    scaling = jnp.where(freq_index == 0, math.sqrt(1.0 / time_count), math.sqrt(2.0 / time_count)).astype(jnp.float32)
    return (scaling[:, None] * jnp.cos(angles), scaling[:, None] * jnp.sin(angles))

def rounded(values):
    return lax.optimization_barrier(values.astype(jnp.bfloat16)).astype(jnp.float32)

def slot_weights(tile_ranks, tile_scales, rank_max):
    slot_index = jnp.arange(rank_max, dtype=jnp.int32)
    live_slots = (slot_index < tile_ranks[..., None]).astype(jnp.float32)
    return (tile_scales[:, 0] * tile_scales[:, 1])[..., None] * live_slots

def forward_one(left, right, weights, wavefield):
    tile_width = left.shape[-1]
    virtual = wavefield.shape[1]
    left_real = left[:, :, 0].astype(jnp.float32)
    left_imag = left[:, :, 1].astype(jnp.float32)
    right_real = right[:, :, 0].astype(jnp.float32)
    right_imag = right[:, :, 1].astype(jnp.float32)
    halves = rounded(wavefield).reshape(2, virtual, right.shape[1], tile_width)

    def project(matrix, vectors):
        return jnp.einsum('ijkp,vjp->ijkv', matrix, vectors)
    coef_real = project(right_real, halves[0]) + project(right_imag, halves[1])
    coef_imag = project(right_real, halves[1]) - project(right_imag, halves[0])
    coeffs = rounded(jnp.stack([coef_real, coef_imag], 2) * weights[:, :, None, :, None])

    def expand(matrix, vectors):
        return jnp.einsum('ijkq,ijkv->viq', matrix, vectors)
    image_real = expand(left_real, coeffs[:, :, 0]) - expand(left_imag, coeffs[:, :, 1])
    image_imag = expand(left_real, coeffs[:, :, 1]) + expand(left_imag, coeffs[:, :, 0])
    return jnp.stack([image_real, image_imag]).reshape(2, virtual, -1)

def adjoint_one(left, right, weights, residual):
    tile_width = left.shape[-1]
    virtual = residual.shape[1]
    left_real = left[:, :, 0].astype(jnp.float32)
    left_imag = left[:, :, 1].astype(jnp.float32)
    right_real = right[:, :, 0].astype(jnp.float32)
    right_imag = right[:, :, 1].astype(jnp.float32)
    halves = rounded(residual).reshape(2, virtual, left.shape[0], tile_width)

    def contract_left(matrix, vectors):
        return jnp.einsum('ijkq,viq->ijkv', matrix, vectors)
    dual_real = contract_left(left_real, halves[0]) + contract_left(left_imag, halves[1])
    dual_imag = contract_left(left_real, halves[1]) - contract_left(left_imag, halves[0])
    duals = rounded(jnp.stack([dual_real, dual_imag], 2) * weights[:, :, None, :, None])

    def spread(matrix, vectors):
        return jnp.einsum('ijkp,ijkv->vjp', matrix, vectors)
    grad_real = spread(right_real, duals[:, :, 0]) - spread(right_imag, duals[:, :, 1])
    grad_imag = spread(right_real, duals[:, :, 1]) + spread(right_imag, duals[:, :, 0])
    return jnp.stack([grad_real, grad_imag]).reshape(2, virtual, -1)

def reference(left_factor, right_factor, tile_ranks, tile_scales, recorded, step_sizes, thresholds):
    weights = slot_weights(tile_ranks, tile_scales, R)
    time_count = 2 * F
    cos_table, sin_table = dft_tables(jnp.arange(F, dtype=jnp.int32), time_count)
    highest = lax.Precision.HIGHEST

    def to_time(wavefield):
        return jnp.einsum('fvn,ft->nvt', wavefield[:, 0], cos_table, precision=highest) - jnp.einsum('fvn,ft->nvt', wavefield[:, 1], sin_table, precision=highest)

    def shrink(signal):
        excess = jnp.abs(signal) - thresholds[None, :, None]
        return jnp.sign(signal) * jnp.maximum(excess, 0.0)

    def to_freq(signal):
        real_part = jnp.einsum('nvt,ft->fvn', signal, cos_table, precision=highest)
        imag_part = -jnp.einsum('nvt,ft->fvn', signal, sin_table, precision=highest)
        return jnp.stack([real_part, imag_part], 1)

    def gradient(residual):
        return lax.map(lambda per_freq: adjoint_one(*per_freq), (left_factor, right_factor, weights, residual))

    def predict(wavefield):
        return lax.map(lambda per_freq: forward_one(*per_freq), (left_factor, right_factor, weights, wavefield))
    scaled = step_sizes[:, None, None, None]
    first = to_freq(shrink(to_time(scaled * gradient(recorded))))
    return to_freq(shrink(to_time(first + scaled * gradient(recorded - predict(first)))))
```

```python
import functools
import math

import jax
import jax.numpy as jnp
import numpy as np
from jax import lax
from jax.experimental import pallas as pl
from jax.experimental.pallas import tpu as pltpu
from jax.sharding import PartitionSpec as P

F = 128


def dft_tables(freq_index, time_count):
    times_row = jnp.arange(time_count, dtype=jnp.int32)
    phase_steps = (freq_index[:, None] * times_row[None, :] % time_count).astype(jnp.float32)
    angles = phase_steps * (2.0 * math.pi / time_count)
    scaling = jnp.where(
        freq_index == 0, math.sqrt(1.0 / time_count), math.sqrt(2.0 / time_count)
    ).astype(jnp.float32)
    return (scaling[:, None] * jnp.cos(angles), scaling[:, None] * jnp.sin(angles))


def slot_weights(tile_ranks, tile_scales, rank_max):
    slot_index = jnp.arange(rank_max, dtype=jnp.int32)
    live_slots = (slot_index < tile_ranks[..., None]).astype(jnp.float32)
    return (tile_scales[:, 0] * tile_scales[:, 1])[..., None] * live_slots


def per_device_plain(
    left_factor, right_factor, tile_ranks, tile_scales, recorded, step_sizes, thresholds
):
    freqs_here = left_factor.shape[0]
    rows_here = left_factor.shape[1]
    col_tiles = left_factor.shape[2]
    rank_max = left_factor.shape[4]
    tile_width = left_factor.shape[5]
    row_tiles = right_factor.shape[1]
    cols_here = right_factor.shape[2]
    virtual = recorded.shape[2]
    tile_pos = lax.axis_index("tile")
    columns_here = cols_here * tile_width
    time_count = 2 * F
    highest = lax.Precision.HIGHEST
    weights = slot_weights(tile_ranks, tile_scales, rank_max)
    weights_right = lax.dynamic_slice_in_dim(weights, tile_pos * cols_here, cols_here, 2)
    weights_left = lax.dynamic_slice_in_dim(weights, tile_pos * rows_here, rows_here, 1)
    left_real = left_factor[:, :, :, 0]
    left_imag = left_factor[:, :, :, 1]
    right_real = right_factor[:, :, :, 0]
    right_imag = right_factor[:, :, :, 1]
    cos_all, sin_all = dft_tables(jnp.arange(F, dtype=jnp.int32), time_count)

    def gradient(residual):
        halves = residual.astype(jnp.bfloat16).reshape(
            freqs_here, 2, virtual, rows_here, tile_width
        )

        def contract_left(matrix, vectors):
            return jnp.einsum(
                "fijkq,fviq->fijkv", matrix, vectors, preferred_element_type=jnp.float32
            )

        dual_real = contract_left(left_real, halves[:, 0]) + contract_left(left_imag, halves[:, 1])
        dual_imag = contract_left(left_real, halves[:, 1]) - contract_left(left_imag, halves[:, 0])
        duals = (
            jnp.stack([dual_real, dual_imag], 3) * weights_left[:, :, :, None, :, None]
        ).astype(jnp.bfloat16)
        duals = duals.reshape(freqs_here, rows_here, col_tiles, 2, rank_max * virtual)
        arrived = lax.all_to_all(duals, "tile", split_axis=2, concat_axis=1, tiled=True)
        arrived = arrived.reshape(freqs_here, row_tiles, cols_here, 2, rank_max, virtual)

        def spread(matrix, vectors):
            return jnp.einsum(
                "fijkp,fijkv->fvjp", matrix, vectors, preferred_element_type=jnp.float32
            )

        grad_real = spread(right_real, arrived[:, :, :, 0]) - spread(
            right_imag, arrived[:, :, :, 1]
        )
        grad_imag = spread(right_real, arrived[:, :, :, 1]) + spread(
            right_imag, arrived[:, :, :, 0]
        )
        return jnp.stack([grad_real, grad_imag], 1).reshape(freqs_here, 2, virtual, columns_here)

    def to_time(wavefield):
        swapped = lax.all_to_all(wavefield, "freq", split_axis=3, concat_axis=0, tiled=True)
        return jnp.einsum("fvn,ft->nvt", swapped[:, 0], cos_all, precision=highest) - jnp.einsum(
            "fvn,ft->nvt", swapped[:, 1], sin_all, precision=highest
        )

    def shrink(signal):
        excess = jnp.abs(signal) - thresholds[None, :, None]
        return jnp.sign(signal) * jnp.maximum(excess, 0.0)

    def to_freq(signal):
        real_part = jnp.einsum("nvt,ft->fvn", signal, cos_all, precision=highest)
        imag_part = -jnp.einsum("nvt,ft->fvn", signal, sin_all, precision=highest)
        return lax.all_to_all(
            jnp.stack([real_part, imag_part], 1), "freq", split_axis=0, concat_axis=3, tiled=True
        )

    scaled = step_sizes[:, None, None, None]
    first = to_freq(shrink(to_time(scaled * gradient(recorded))))
    halves = first.astype(jnp.bfloat16).reshape(freqs_here, 2, virtual, cols_here, tile_width)

    def project(matrix, vectors):
        return jnp.einsum("fijkp,fvjp->fijkv", matrix, vectors, preferred_element_type=jnp.float32)

    coef_real = project(right_real, halves[:, 0]) + project(right_imag, halves[:, 1])
    coef_imag = project(right_real, halves[:, 1]) - project(right_imag, halves[:, 0])
    coeffs = (jnp.stack([coef_real, coef_imag], 3) * weights_right[:, :, :, None, :, None]).astype(
        jnp.bfloat16
    )
    coeffs = coeffs.reshape(freqs_here, row_tiles, cols_here, 2, rank_max * virtual)
    arrived = lax.all_to_all(coeffs, "tile", split_axis=1, concat_axis=2, tiled=True)
    arrived = arrived.reshape(freqs_here, rows_here, col_tiles, 2, rank_max, virtual)

    def expand(matrix, vectors):
        return jnp.einsum("fijkq,fijkv->fviq", matrix, vectors, preferred_element_type=jnp.float32)

    image_real = expand(left_real, arrived[:, :, :, 0]) - expand(left_imag, arrived[:, :, :, 1])
    image_imag = expand(left_real, arrived[:, :, :, 1]) + expand(left_imag, arrived[:, :, :, 0])
    return to_freq(
        shrink(
            to_time(
                first
                + scaled
                * gradient(
                    recorded
                    - jnp.stack([image_real, image_imag], 1).reshape(
                        freqs_here, 2, virtual, rows_here * tile_width
                    )
                )
            )
        )
    )


def swap_parts(values, first_part, half):
    pieces = []
    for start in range(0, values.shape[1], 128):
        piece = values[:, start : start + 128]
        pieces.append(
            jnp.where(
                first_part, pltpu.roll(piece, 128 - half, 1), pltpu.roll(piece, half, 1)
            )
        )
    return jnp.concatenate(pieces, 1)


def lane_ids(rows, lanes):
    return lax.broadcasted_iota(jnp.int32, (rows, lanes), 1)


def adjoint_rows(product, half):
    virtual = product.shape[0] // 2
    lanes = product.shape[1]
    sign = jnp.where(lane_ids(virtual, lanes) // half % 2 == 0, 1.0, -1.0)
    first_part = lane_ids(virtual, 128) // half % 2 == 0
    return product[:virtual] * sign + swap_parts(product[virtual:], first_part, half)


def forward_rows(coefs, half):
    rows, lanes = coefs.shape
    sign = jnp.where(lane_ids(rows, lanes) // half % 2 == 0, 1.0, -1.0)
    first_part = lane_ids(rows, 128) // half % 2 == 0
    return coefs * sign, swap_parts(coefs, first_part, half)


def nt_dot(a, b):
    return lax.dot_general(a, b, (((1,), (1,)), ((), ())), preferred_element_type=jnp.float32)


def nn_dot(a, b):
    return jnp.dot(a, b, preferred_element_type=jnp.float32)


def dual_of(left_rows, field, weight, half):
    return adjoint_rows(nt_dot(field.astype(jnp.bfloat16), left_rows), half) * weight


def store_duals(out_ref, at, duals, peers):
    together = jnp.concatenate(duals, 0)
    width = together.shape[1] // peers
    for peer in range(peers):
        out_ref[peer, at] = together[:, peer * width : (peer + 1) * width].astype(jnp.bfloat16)


def dual_kernel(left_ref, recorded_ref, weight_ref, out_ref):
    freqs, rows, cols, _, rank, width = left_ref.shape
    peers = out_ref.shape[0]
    for at in range(freqs):
        duals = []
        for row in range(rows):
            left_rows = left_ref[at, row].reshape(cols * 2 * rank, width)
            part = recorded_ref[at, :, :, row * width : (row + 1) * width]
            field = part.reshape(-1, width)
            duals.append(dual_of(left_rows, field, weight_ref[at, row : row + 1], rank))
        store_duals(out_ref, at, duals, peers)


def image_kernel(left_ref, coefs_ref, recorded_ref, weight_ref, out_ref):
    freqs, rows, cols, _, rank, width = left_ref.shape
    peers = coefs_ref.shape[0]
    share = cols // peers * 2 * rank
    virtual = recorded_ref.shape[2]
    for at in range(freqs):
        forms = [
            forward_rows(coefs_ref[peer, at].astype(jnp.float32), rank) for peer in range(peers)
        ]
        duals = []
        for row in range(rows):
            left_rows = left_ref[at, row].reshape(cols * 2 * rank, width)
            own = slice(row * virtual, (row + 1) * virtual)
            image = 0.0
            for peer, (real_form, imag_form) in enumerate(forms):
                both = jnp.concatenate([real_form[own], imag_form[own]], 0).astype(jnp.bfloat16)
                image += nn_dot(both, left_rows[peer * share : (peer + 1) * share])
            part = recorded_ref[at, :, :, row * width : (row + 1) * width]
            field = part.reshape(-1, width) - image
            duals.append(dual_of(left_rows, field, weight_ref[at, row : row + 1], rank))
        store_duals(out_ref, at, duals, peers)


def spread_kernel(steps_ref, right_ref, duals_ref, out_ref):
    freqs, rows, cols, _, rank, width = right_ref.shape
    peers, _, both, share = duals_ref.shape
    rows_each = rows // peers
    virtual = both // rows_each
    group = 2 * rank
    owner = lane_ids(2 * virtual, share) // group
    for at in range(freqs):
        wide = []
        for peer in range(peers):
            real_form, imag_form = forward_rows(duals_ref[peer, at].astype(jnp.float32), rank)
            for row in range(rows_each):
                own = slice(row * virtual, (row + 1) * virtual)
                rows_both = jnp.concatenate([real_form[own], imag_form[own]], 0)
                wide.append(
                    jnp.concatenate(
                        [jnp.where(owner == col, rows_both, 0.0) for col in range(cols)], 0
                    ).astype(jnp.bfloat16)
                )
        total = 0.0
        for row in range(rows):
            total += nn_dot(wide[row], right_ref[at, row].reshape(cols * group, width))
        step = steps_ref[pl.program_id(0) * freqs + at]
        out_ref[:, at] = (total * step).astype(jnp.bfloat16).reshape(cols, 2 * virtual, width)


def project_kernel(right_ref, field_ref, weight_ref, out_ref):
    freqs, rows, cols, _, rank, width = right_ref.shape
    peers, _, both, share = out_ref.shape
    rows_each = rows // peers
    virtual = both // rows_each
    group = 2 * rank
    owner = lane_ids(2 * virtual, 128) // group
    per_piece = 128 // group
    for at in range(freqs):
        field = field_ref[:, at].reshape(cols * 2 * virtual, width)
        for peer in range(peers):
            coefs = []
            for row in range(peer * rows_each, (peer + 1) * rows_each):
                product = nt_dot(field, right_ref[at, row].reshape(cols * group, width))
                pieces = []
                for start in range(0, share, 128):
                    piece = 0.0
                    for step in range(per_piece):
                        col = start // group + step
                        rows_of = product[
                            col * 2 * virtual : (col + 1) * 2 * virtual, start : start + 128
                        ]
                        piece = rows_of if step == 0 else jnp.where(owner == step, rows_of, piece)
                    pieces.append(piece)
                picked = jnp.concatenate(pieces, 1)
                coefs.append(adjoint_rows(picked, rank) * weight_ref[at, row : row + 1])
            out_ref[peer, at] = jnp.concatenate(coefs, 0).astype(jnp.bfloat16)


def split_two(values):
    high = values.astype(jnp.bfloat16)
    return high, (values - high.astype(jnp.float32)).astype(jnp.bfloat16)


def shrink_kernel(second, *refs):
    if second:
        (levels_ref, to_high, to_low, back_high, back_low, field_ref, kept_ref, out_ref,
         wide, packed) = refs
    else:
        (levels_ref, to_high, to_low, back_high, back_low, field_ref, out_ref, kept_ref,
         wide, packed) = refs
    virtual = levels_ref.shape[0]
    peers, freqs, rows, width = field_ref.shape
    times = to_high.shape[0]
    lines = peers * freqs * 2
    halves = [slice(at, at + 128) for at in range(0, width, 128)]
    for half, lanes in enumerate(halves):
        wide[half] = (
            field_ref[:, :, :, lanes].astype(jnp.float32).reshape(lines * virtual, 128)
        )
    if not second:
        odd = lax.broadcasted_iota(jnp.int32, (times, width), 0) % 2
        turn = jnp.where(odd == 0, 1.0, -1.0)
    for source in range(virtual):
        own = pl.ds(source, lines, stride=virtual)
        spectrum = jnp.concatenate(
            [wide[half, own, :] for half in range(len(halves))], 1
        ).astype(jnp.bfloat16)
        signal = nn_dot(to_high[...], spectrum) + nn_dot(to_low[...], spectrum)
        if second:
            signal += kept_ref[source]
        level = levels_ref[source]
        shrunk = signal - jnp.clip(signal, -level, level)
        if not second:
            mean = jnp.sum(shrunk * turn, 0, keepdims=True) * (1.0 / times)
            kept_ref[source] = shrunk - turn * mean
        high, low = split_two(shrunk)
        freq = nn_dot(back_high[...], high) + nn_dot(back_low[...], high) + nn_dot(
            back_high[...], low
        )
        for half, lanes in enumerate(halves):
            packed[half, own, :] = freq[:, lanes]
    for half, lanes in enumerate(halves):
        out_ref[:, :, :, lanes] = (
            packed[half].astype(jnp.bfloat16).reshape(peers, freqs, rows, 128)
        )


def table_parts():
    times = 2 * F
    freq = np.arange(F)[:, None]
    angles = (freq * np.arange(times)[None, :] % times) * (2.0 * math.pi / times)
    scaling = np.where(freq == 0, math.sqrt(1.0 / times), math.sqrt(2.0 / times))
    table = np.stack([scaling * np.cos(angles), -scaling * np.sin(angles)], 1)
    table = table.reshape(2 * F, times).astype(np.float32)
    high = table.astype(jnp.bfloat16)
    low = (table - high.astype(np.float32)).astype(jnp.bfloat16)
    return tuple(jnp.asarray(part) for part in (high.T, low.T, high, low))


def vmem():
    return pl.BlockSpec(memory_space=pltpu.VMEM)


def smem():
    return pl.BlockSpec(memory_space=pltpu.SMEM)


PARAMS = pltpu.CompilerParams(vmem_limit_bytes=48 << 20, dimension_semantics=("arbitrary",))


def per_device(
    left_factor, right_factor, tile_ranks, tile_scales, recorded, step_sizes, thresholds
):
    freqs, rows_here, col_tiles, _, rank, width = left_factor.shape
    row_tiles, cols_here = right_factor.shape[1:3]
    virtual = recorded.shape[2]
    tile_size = col_tiles // cols_here
    share = cols_here * 2 * rank
    lines = rows_here * virtual
    tile_pos = lax.axis_index("tile")
    block = 2 if freqs % 2 == 0 else 1
    grid = (freqs // block,)

    weights = slot_weights(tile_ranks, tile_scales, rank)
    weights = jnp.broadcast_to(
        weights[:, :, :, None, :], (freqs, row_tiles, col_tiles, 2, rank)
    ).reshape(freqs, row_tiles, col_tiles * 2 * rank)
    weights_left = lax.dynamic_slice_in_dim(weights, tile_pos * rows_here, rows_here, 1)
    weights_right = lax.dynamic_slice_in_dim(weights, tile_pos * share, share, 2)

    def by_freq(array):
        rest = array.shape[1:]
        return pl.BlockSpec((block,) + rest, lambda f: (f,) + (0,) * len(rest))

    def by_second(shape):
        return pl.BlockSpec((shape[0], block) + shape[2:], lambda f: (0, f, 0, 0))

    coef_shape = (tile_size, freqs, lines, share)
    field_shape = (cols_here, freqs, 2 * virtual, width)
    coef_type = jax.ShapeDtypeStruct(coef_shape, jnp.bfloat16)
    field_type = jax.ShapeDtypeStruct(field_shape, jnp.bfloat16)

    def spread(duals):
        return pl.pallas_call(
            spread_kernel,
            out_shape=field_type,
            grid=grid,
            in_specs=[smem(), by_freq(right_factor), by_second(coef_shape)],
            out_specs=by_second(field_shape),
            compiler_params=PARAMS,
        )(step_sizes, right_factor, duals)

    def over_tile(array):
        return lax.all_to_all(array, "tile", split_axis=0, concat_axis=0, tiled=True)

    def over_freq(array):
        return lax.all_to_all(array, "freq", split_axis=0, concat_axis=0, tiled=True)

    times = 2 * F
    kept_type = jax.ShapeDtypeStruct((virtual, times, width), jnp.float32)
    tables = table_parts()
    scratch = [pltpu.VMEM((width // 128, times * virtual, 128), jnp.float32)] * 2

    duals = pl.pallas_call(
        dual_kernel,
        out_shape=coef_type,
        grid=grid,
        in_specs=[by_freq(left_factor), by_freq(recorded), by_freq(weights_left)],
        out_specs=by_second(coef_shape),
        compiler_params=PARAMS,
    )(left_factor, recorded, weights_left)
    gradient = over_freq(spread(over_tile(duals)))
    first, kept = pl.pallas_call(
        functools.partial(shrink_kernel, False),
        out_shape=[field_type, kept_type],
        in_specs=[smem()] + [vmem()] * 5,
        out_specs=[vmem(), vmem()],
        scratch_shapes=scratch,
        compiler_params=pltpu.CompilerParams(vmem_limit_bytes=48 << 20),
    )(thresholds, *tables, gradient)
    coefs = pl.pallas_call(
        project_kernel,
        out_shape=coef_type,
        grid=grid,
        in_specs=[by_freq(right_factor), by_second(field_shape), by_freq(weights_right)],
        out_specs=by_second(coef_shape),
        compiler_params=PARAMS,
    )(right_factor, over_freq(first), weights_right)
    duals = pl.pallas_call(
        image_kernel,
        out_shape=coef_type,
        grid=grid,
        in_specs=[
            by_freq(left_factor),
            by_second(coef_shape),
            by_freq(recorded),
            by_freq(weights_left),
        ],
        out_specs=by_second(coef_shape),
        compiler_params=PARAMS,
    )(left_factor, over_tile(coefs), recorded, weights_left)
    gradient = over_freq(spread(over_tile(duals)))
    estimate = pl.pallas_call(
        functools.partial(shrink_kernel, True),
        out_shape=field_type,
        in_specs=[smem()] + [vmem()] * 6,
        out_specs=vmem(),
        scratch_shapes=scratch,
        compiler_params=pltpu.CompilerParams(vmem_limit_bytes=48 << 20),
    )(thresholds, *tables, gradient, kept)
    arrived = over_freq(estimate).astype(jnp.float32)
    return arrived.transpose(1, 2, 0, 3).reshape(freqs, 2, virtual, cols_here * width)


def either(*arrays):
    left_factor, right_factor = arrays[:2]
    cols_here = right_factor.shape[2]
    rank, width = left_factor.shape[4:]
    aligned = (
        cols_here == lax.axis_size("freq")
        and width % 128 == 0
        and 128 % (2 * rank) == 0
        and (cols_here * 2 * rank) % 128 == 0
        and arrays[4].shape[2] == 8
        and left_factor.shape[0] * lax.axis_size("freq") == F
    )
    return (per_device if aligned else per_device_plain)(*arrays)


def solution(mesh):
    return jax.shard_map(
        either,
        mesh=mesh,
        in_specs=(
            P("freq", "tile", None, None, None, None),
            P("freq", None, "tile", None, None, None),
            P("freq", None, None),
            P("freq", None, None, None),
            P("freq", None, None, "tile"),
            P("freq"),
            P(),
        ),
        out_specs=P("freq", None, None, "tile"),
        check_vma=False,
    )
```

```python
import functools
import math

import jax
import jax.numpy as jnp
import numpy as np
from jax import lax
from jax.experimental import pallas as pl
from jax.experimental.pallas import tpu as pltpu
from jax.sharding import PartitionSpec as P

F = 128


def dft_tables(freq_index, time_count):
    times_row = jnp.arange(time_count, dtype=jnp.int32)
    phase_steps = (freq_index[:, None] * times_row[None, :] % time_count).astype(jnp.float32)
    angles = phase_steps * (2.0 * math.pi / time_count)
    scaling = jnp.where(
        freq_index == 0, math.sqrt(1.0 / time_count), math.sqrt(2.0 / time_count)
    ).astype(jnp.float32)
    return (scaling[:, None] * jnp.cos(angles), scaling[:, None] * jnp.sin(angles))


def slot_weights(tile_ranks, tile_scales, rank_max):
    slot_index = jnp.arange(rank_max, dtype=jnp.int32)
    live_slots = (slot_index < tile_ranks[..., None]).astype(jnp.float32)
    return (tile_scales[:, 0] * tile_scales[:, 1])[..., None] * live_slots


def per_device_plain(
    left_factor, right_factor, tile_ranks, tile_scales, recorded, step_sizes, thresholds
):
    freqs_here = left_factor.shape[0]
    rows_here = left_factor.shape[1]
    col_tiles = left_factor.shape[2]
    rank_max = left_factor.shape[4]
    tile_width = left_factor.shape[5]
    row_tiles = right_factor.shape[1]
    cols_here = right_factor.shape[2]
    virtual = recorded.shape[2]
    tile_pos = lax.axis_index("tile")
    columns_here = cols_here * tile_width
    time_count = 2 * F
    highest = lax.Precision.HIGHEST
    weights = slot_weights(tile_ranks, tile_scales, rank_max)
    weights_right = lax.dynamic_slice_in_dim(weights, tile_pos * cols_here, cols_here, 2)
    weights_left = lax.dynamic_slice_in_dim(weights, tile_pos * rows_here, rows_here, 1)
    left_real = left_factor[:, :, :, 0]
    left_imag = left_factor[:, :, :, 1]
    right_real = right_factor[:, :, :, 0]
    right_imag = right_factor[:, :, :, 1]
    cos_all, sin_all = dft_tables(jnp.arange(F, dtype=jnp.int32), time_count)

    def gradient(residual):
        halves = residual.astype(jnp.bfloat16).reshape(
            freqs_here, 2, virtual, rows_here, tile_width
        )

        def contract_left(matrix, vectors):
            return jnp.einsum(
                "fijkq,fviq->fijkv", matrix, vectors, preferred_element_type=jnp.float32
            )

        dual_real = contract_left(left_real, halves[:, 0]) + contract_left(left_imag, halves[:, 1])
        dual_imag = contract_left(left_real, halves[:, 1]) - contract_left(left_imag, halves[:, 0])
        duals = (
            jnp.stack([dual_real, dual_imag], 3) * weights_left[:, :, :, None, :, None]
        ).astype(jnp.bfloat16)
        duals = duals.reshape(freqs_here, rows_here, col_tiles, 2, rank_max * virtual)
        arrived = lax.all_to_all(duals, "tile", split_axis=2, concat_axis=1, tiled=True)
        arrived = arrived.reshape(freqs_here, row_tiles, cols_here, 2, rank_max, virtual)

        def spread(matrix, vectors):
            return jnp.einsum(
                "fijkp,fijkv->fvjp", matrix, vectors, preferred_element_type=jnp.float32
            )

        grad_real = spread(right_real, arrived[:, :, :, 0]) - spread(
            right_imag, arrived[:, :, :, 1]
        )
        grad_imag = spread(right_real, arrived[:, :, :, 1]) + spread(
            right_imag, arrived[:, :, :, 0]
        )
        return jnp.stack([grad_real, grad_imag], 1).reshape(freqs_here, 2, virtual, columns_here)

    def to_time(wavefield):
        swapped = lax.all_to_all(wavefield, "freq", split_axis=3, concat_axis=0, tiled=True)
        return jnp.einsum("fvn,ft->nvt", swapped[:, 0], cos_all, precision=highest) - jnp.einsum(
            "fvn,ft->nvt", swapped[:, 1], sin_all, precision=highest
        )

    def shrink(signal):
        excess = jnp.abs(signal) - thresholds[None, :, None]
        return jnp.sign(signal) * jnp.maximum(excess, 0.0)

    def to_freq(signal):
        real_part = jnp.einsum("nvt,ft->fvn", signal, cos_all, precision=highest)
        imag_part = -jnp.einsum("nvt,ft->fvn", signal, sin_all, precision=highest)
        return lax.all_to_all(
            jnp.stack([real_part, imag_part], 1), "freq", split_axis=0, concat_axis=3, tiled=True
        )

    scaled = step_sizes[:, None, None, None]
    first = to_freq(shrink(to_time(scaled * gradient(recorded))))
    halves = first.astype(jnp.bfloat16).reshape(freqs_here, 2, virtual, cols_here, tile_width)

    def project(matrix, vectors):
        return jnp.einsum("fijkp,fvjp->fijkv", matrix, vectors, preferred_element_type=jnp.float32)

    coef_real = project(right_real, halves[:, 0]) + project(right_imag, halves[:, 1])
    coef_imag = project(right_real, halves[:, 1]) - project(right_imag, halves[:, 0])
    coeffs = (jnp.stack([coef_real, coef_imag], 3) * weights_right[:, :, :, None, :, None]).astype(
        jnp.bfloat16
    )
    coeffs = coeffs.reshape(freqs_here, row_tiles, cols_here, 2, rank_max * virtual)
    arrived = lax.all_to_all(coeffs, "tile", split_axis=1, concat_axis=2, tiled=True)
    arrived = arrived.reshape(freqs_here, rows_here, col_tiles, 2, rank_max, virtual)

    def expand(matrix, vectors):
        return jnp.einsum("fijkq,fijkv->fviq", matrix, vectors, preferred_element_type=jnp.float32)

    image_real = expand(left_real, arrived[:, :, :, 0]) - expand(left_imag, arrived[:, :, :, 1])
    image_imag = expand(left_real, arrived[:, :, :, 1]) + expand(left_imag, arrived[:, :, :, 0])
    return to_freq(
        shrink(
            to_time(
                first
                + scaled
                * gradient(
                    recorded
                    - jnp.stack([image_real, image_imag], 1).reshape(
                        freqs_here, 2, virtual, rows_here * tile_width
                    )
                )
            )
        )
    )


def swap_parts(values, first_part, half):
    pieces = []
    for start in range(0, values.shape[1], 128):
        piece = values[:, start : start + 128]
        pieces.append(
            jnp.where(
                first_part, pltpu.roll(piece, 128 - half, 1), pltpu.roll(piece, half, 1)
            )
        )
    return jnp.concatenate(pieces, 1)


def lane_ids(rows, lanes):
    return lax.broadcasted_iota(jnp.int32, (rows, lanes), 1)


def adjoint_rows(product, half):
    virtual = product.shape[0] // 2
    lanes = product.shape[1]
    sign = jnp.where(lane_ids(virtual, lanes) // half % 2 == 0, 1.0, -1.0)
    first_part = lane_ids(virtual, 128) // half % 2 == 0
    return product[:virtual] * sign + swap_parts(product[virtual:], first_part, half)


def forward_rows(coefs, half):
    rows, lanes = coefs.shape
    sign = jnp.where(lane_ids(rows, lanes) // half % 2 == 0, 1.0, -1.0)
    first_part = lane_ids(rows, 128) // half % 2 == 0
    return coefs * sign, swap_parts(coefs, first_part, half)


def nt_dot(a, b):
    return lax.dot_general(a, b, (((1,), (1,)), ((), ())), preferred_element_type=jnp.float32)


def nn_dot(a, b):
    return jnp.dot(a, b, preferred_element_type=jnp.float32)


def dual_of(left_rows, field, weight, half):
    return adjoint_rows(nt_dot(field.astype(jnp.bfloat16), left_rows), half) * weight


def store_duals(out_ref, at, duals, peers):
    together = jnp.concatenate(duals, 0)
    width = together.shape[1] // peers
    for peer in range(peers):
        out_ref[peer, at] = together[:, peer * width : (peer + 1) * width].astype(jnp.bfloat16)


def dual_kernel(left_ref, recorded_ref, weight_ref, out_ref):
    freqs, rows, cols, _, rank, width = left_ref.shape
    peers = out_ref.shape[0]
    for at in range(freqs):
        duals = []
        for row in range(rows):
            left_rows = left_ref[at, row].reshape(cols * 2 * rank, width)
            part = recorded_ref[at, :, :, row * width : (row + 1) * width]
            field = part.reshape(-1, width)
            duals.append(dual_of(left_rows, field, weight_ref[at, row : row + 1], rank))
        store_duals(out_ref, at, duals, peers)


def image_kernel(left_ref, coefs_ref, recorded_ref, weight_ref, out_ref):
    freqs, rows, cols, _, rank, width = left_ref.shape
    peers = coefs_ref.shape[0]
    share = cols // peers * 2 * rank
    virtual = recorded_ref.shape[2]
    for at in range(freqs):
        forms = [
            forward_rows(coefs_ref[peer, at].astype(jnp.float32), rank) for peer in range(peers)
        ]
        duals = []
        for row in range(rows):
            left_rows = left_ref[at, row].reshape(cols * 2 * rank, width)
            own = slice(row * virtual, (row + 1) * virtual)
            image = 0.0
            for peer, (real_form, imag_form) in enumerate(forms):
                both = jnp.concatenate([real_form[own], imag_form[own]], 0).astype(jnp.bfloat16)
                image += nn_dot(both, left_rows[peer * share : (peer + 1) * share])
            part = recorded_ref[at, :, :, row * width : (row + 1) * width]
            field = part.reshape(-1, width) - image
            duals.append(dual_of(left_rows, field, weight_ref[at, row : row + 1], rank))
        store_duals(out_ref, at, duals, peers)


def spread_kernel(base, steps_ref, right_ref, duals_ref, out_ref):
    freqs, rows, cols, _, rank, width = right_ref.shape
    peers, _, both, share = duals_ref.shape
    rows_each = rows // peers
    virtual = both // rows_each
    group = 2 * rank
    owner = lane_ids(2 * virtual, share) // group
    for at in range(freqs):
        wide = []
        for peer in range(peers):
            real_form, imag_form = forward_rows(duals_ref[peer, at].astype(jnp.float32), rank)
            for row in range(rows_each):
                own = slice(row * virtual, (row + 1) * virtual)
                rows_both = jnp.concatenate([real_form[own], imag_form[own]], 0)
                wide.append(
                    jnp.concatenate(
                        [jnp.where(owner == col, rows_both, 0.0) for col in range(cols)], 0
                    ).astype(jnp.bfloat16)
                )
        total = 0.0
        for row in range(rows):
            total += nn_dot(wide[row], right_ref[at, row].reshape(cols * group, width))
        step = steps_ref[base + at]
        out_ref[:, at] = (total * step).astype(jnp.bfloat16).reshape(cols, 2 * virtual, width)


def project_kernel(right_ref, field_ref, weight_ref, out_ref):
    freqs, rows, cols, _, rank, width = right_ref.shape
    peers, _, both, share = out_ref.shape
    rows_each = rows // peers
    virtual = both // rows_each
    group = 2 * rank
    owner = lane_ids(2 * virtual, 128) // group
    per_piece = 128 // group
    for at in range(freqs):
        field = field_ref[:, at].reshape(cols * 2 * virtual, width)
        for peer in range(peers):
            coefs = []
            for row in range(peer * rows_each, (peer + 1) * rows_each):
                product = nt_dot(field, right_ref[at, row].reshape(cols * group, width))
                pieces = []
                for start in range(0, share, 128):
                    piece = 0.0
                    for step in range(per_piece):
                        col = start // group + step
                        rows_of = product[
                            col * 2 * virtual : (col + 1) * 2 * virtual, start : start + 128
                        ]
                        piece = rows_of if step == 0 else jnp.where(owner == step, rows_of, piece)
                    pieces.append(piece)
                picked = jnp.concatenate(pieces, 1)
                coefs.append(adjoint_rows(picked, rank) * weight_ref[at, row : row + 1])
            out_ref[peer, at] = jnp.concatenate(coefs, 0).astype(jnp.bfloat16)


def split_two(values):
    high = values.astype(jnp.bfloat16)
    return high, (values - high.astype(jnp.float32)).astype(jnp.bfloat16)


def shrink_kernel(second, levels_ref, tables, field_ref, kept_ref, out_ref, wide, packed):
    to_high, to_low, back_high, back_low = tables
    virtual = levels_ref.shape[0]
    width = field_ref.shape[-1]
    times, lines = to_high.shape
    halves = [slice(at, at + 128) for at in range(0, width, 128)]
    for half, lanes in enumerate(halves):
        wide[half] = (
            field_ref[:, :, :, :, lanes].astype(jnp.float32).reshape(lines * virtual, 128)
        )
    odd = lax.broadcasted_iota(jnp.int32, (times, width), 0) % 2
    turn = jnp.where(odd == 0, 1.0, -1.0)
    for source in range(virtual):
        own = pl.ds(source, lines, stride=virtual)
        spectrum = jnp.concatenate(
            [wide[half, own, :] for half in range(len(halves))], 1
        ).astype(jnp.bfloat16)
        signal = nn_dot(to_high[...], spectrum) + nn_dot(to_low[...], spectrum)
        if second:
            signal += kept_ref[source]
        level = levels_ref[source]
        shrunk = signal - jnp.minimum(jnp.maximum(signal, -level), level)
        if not second:
            mean = jnp.sum(shrunk * turn, 0, keepdims=True) * (1.0 / times)
            kept_ref[source] = shrunk - turn * mean
        high, low = split_two(shrunk)
        freq = nn_dot(back_high[...], high) + nn_dot(back_low[...], high) + nn_dot(
            back_high[...], low
        )
        for half, lanes in enumerate(halves):
            packed[half, own, :] = freq[:, lanes]
    for half, lanes in enumerate(halves):
        out_ref[:, :, :, :, lanes] = (
            packed[half].astype(jnp.bfloat16).reshape(out_ref.shape[:-1] + (128,))
        )


class Exchange:
    def __init__(self, axis, send, recv, send_sem, recv_sem):
        self.axis, self.send, self.recv = axis, send, recv
        self.send_sem, self.recv_sem = send_sem, recv_sem
        self.size = send.shape[0]
        self.me = lax.axis_index(axis)

    def peers(self):
        return [lax.rem(self.me + step, self.size) for step in range(1, self.size)]

    def copy(self, block, peer, source):
        return pltpu.make_async_remote_copy(
            src_ref=self.send.at[peer, block],
            dst_ref=self.recv.at[source, block],
            send_sem=self.send_sem.at[block, peer],
            recv_sem=self.recv_sem.at[block, source],
            device_id={self.axis: peer},
            device_id_type=pl.DeviceIdType.MESH,
        )

    def start(self, block):
        for peer in self.peers():
            self.copy(block, peer, self.me).start()
        self.recv[self.me, block] = self.send[self.me, block]

    def start_all(self):
        @pl.loop(0, self.send.shape[1])
        def _(block):
            self.start(block)

    def wait(self, block):
        for peer in self.peers():
            self.copy(block, peer, peer).wait_recv()

    def wait_all(self):
        @pl.loop(0, self.send.shape[1])
        def _(block):
            self.wait(block)

    def finish(self):
        @pl.loop(0, self.send.shape[1])
        def _(block):
            for peer in self.peers():
                self.copy(block, peer, self.me).wait_send()


def stages(blocks):
    lag = LAG
    first_shrink = blocks + lag
    second_shrink = first_shrink + blocks + 2 * lag
    return lag, first_shrink, second_shrink, second_shrink + blocks


def whole_kernel(
    levels_ref, steps_ref, to_high, to_low, back_high, back_low,
    left_ref, recorded_ref, weight_left_ref, right_a_ref, weight_right_ref, right_b_ref,
    out_ref,
    tile_send, tile_recv, freq_send, freq_recv, tile_ssem, tile_rsem, freq_ssem, freq_rsem,
    kept, wide, packed,
):
    step = pl.program_id(0)
    block = left_ref.shape[0]
    blocks = tile_send.shape[2]
    lag, first_shrink, second_shrink, last = stages(blocks)
    tables = (to_high, to_low, back_high, back_low)
    over_tile = [
        Exchange("tile", tile_send.at[n], tile_recv.at[n], tile_ssem.at[n], tile_rsem.at[n])
        for n in range(tile_send.shape[0])
    ]
    over_freq = [
        Exchange("freq", freq_send.at[n], freq_recv.at[n], freq_ssem.at[n], freq_rsem.at[n])
        for n in range(freq_send.shape[0])
    ]

    def span(start):
        return (step >= start) & (step < start + blocks)

    @pl.when(step == 0)
    def _():
        barrier = pltpu.get_barrier_semaphore()
        count = 0
        for exchange in (over_tile[0], over_freq[0]):
            for peer in exchange.peers():
                pl.semaphore_signal(
                    barrier, inc=1, device_id={exchange.axis: peer},
                    device_id_type=pl.DeviceIdType.MESH,
                )
                count += 1
        pl.semaphore_wait(barrier, count)

    @pl.when(span(0))
    def _():
        dual_kernel(left_ref, recorded_ref, weight_left_ref, over_tile[0].send.at[:, step])
        over_tile[0].start(step)

    def spread(start, tiles, freqs):
        @pl.when(span(start))
        def _():
            b = step - start
            tiles.wait(b)
            spread_kernel(
                b * block, steps_ref, right_b_ref, tiles.recv.at[:, b], freqs.send.at[:, b]
            )
            freqs.start(b)

    spread(lag, over_tile[0], over_freq[0])

    @pl.when(step == first_shrink)
    def _():
        over_freq[0].wait_all()
        shrink_kernel(
            False, levels_ref, tables, over_freq[0].recv, kept, over_freq[1].send, wide, packed
        )
        over_freq[1].start_all()

    @pl.when(span(first_shrink))
    def _():
        b = step - first_shrink
        over_freq[1].wait(b)
        project_kernel(
            right_a_ref, over_freq[1].recv.at[:, b], weight_right_ref,
            over_tile[1].send.at[:, b],
        )
        over_tile[1].start(b)

    @pl.when(span(first_shrink + lag))
    def _():
        b = step - first_shrink - lag
        over_tile[1].wait(b)
        image_kernel(
            left_ref, over_tile[1].recv.at[:, b], recorded_ref, weight_left_ref,
            over_tile[2].send.at[:, b],
        )
        over_tile[2].start(b)

    spread(first_shrink + 2 * lag, over_tile[2], over_freq[2])

    @pl.when(step == second_shrink)
    def _():
        over_freq[2].wait_all()
        shrink_kernel(
            True, levels_ref, tables, over_freq[2].recv, kept, over_freq[3].send, wide, packed
        )
        over_freq[3].start_all()

    @pl.when(span(second_shrink))
    def _():
        b = step - second_shrink
        over_freq[3].wait(b)
        peers, _, at_once, rows, width = over_freq[3].recv.shape
        for at in range(at_once):
            for peer in range(peers):
                out_ref[at, :, peer * width : (peer + 1) * width] = over_freq[3].recv[
                    peer, b, at
                ].astype(jnp.float32)

    @pl.when(step == last - 1)
    def _():
        for exchange in over_tile + over_freq:
            exchange.finish()


LAG = 2


def table_parts():
    times = 2 * F
    freq = np.arange(F)[:, None]
    angles = (freq * np.arange(times)[None, :] % times) * (2.0 * math.pi / times)
    scaling = np.where(freq == 0, math.sqrt(1.0 / times), math.sqrt(2.0 / times))
    table = np.stack([scaling * np.cos(angles), -scaling * np.sin(angles)], 1)
    table = table.reshape(2 * F, times).astype(np.float32)
    high = table.astype(jnp.bfloat16)
    low = (table - high.astype(np.float32)).astype(jnp.bfloat16)
    return tuple(jnp.asarray(part) for part in (high.T, low.T, high, low))


def vmem():
    return pl.BlockSpec(memory_space=pltpu.VMEM)


def smem():
    return pl.BlockSpec(memory_space=pltpu.SMEM)


def per_device(
    left_factor, right_factor, tile_ranks, tile_scales, recorded, step_sizes, thresholds
):
    freqs, rows_here, col_tiles, _, rank, width = left_factor.shape
    row_tiles, cols_here = right_factor.shape[1:3]
    virtual = recorded.shape[2]
    tile_size = col_tiles // cols_here
    share = cols_here * 2 * rank
    lines = rows_here * virtual
    tile_pos = lax.axis_index("tile")
    block = 2 if freqs % 2 == 0 else 1
    blocks = freqs // block
    lag, first_shrink, second_shrink, steps = stages(blocks)

    def slot_lanes(row_at, rows, col_at, cols):
        ranks = tile_ranks.astype(jnp.float32)
        scales = tile_scales[:, 0] * tile_scales[:, 1]
        cut = lambda array: lax.dynamic_slice(array, (0, row_at, col_at), (freqs, rows, cols))
        lanes = np.arange(cols * 2 * rank)
        spread_out = jnp.asarray(
            (lanes[None, :] // (2 * rank) == np.arange(cols)[:, None]).astype(np.float32)
        )
        widen = lambda array: jnp.einsum(
            "fij,jl->fil", cut(array), spread_out, precision=lax.Precision.HIGHEST
        )
        slot = (jnp.arange(cols * 2 * rank) % rank).astype(jnp.float32)
        return jnp.where(slot < widen(ranks) - 0.5, widen(scales), 0.0)

    weights_left = slot_lanes(tile_pos * rows_here, rows_here, 0, col_tiles)
    weights_right = slot_lanes(0, row_tiles, tile_pos * cols_here, cols_here)

    def spec(array, index):
        rest = array.shape[1:]
        return pl.BlockSpec((block,) + rest, lambda s: (index(s),) + (0,) * len(rest))

    def within(at):
        return jnp.minimum(jnp.maximum(at, 0), blocks - 1)

    def left_index(s):
        return jnp.where(s < blocks, s, within(s - first_shrink - lag))

    def project_index(s):
        return within(s - first_shrink)

    def spread_index(s):
        return jnp.where(s < first_shrink, within(s - lag), within(s - first_shrink - 2 * lag))

    def out_index(s):
        return within(s - second_shrink)

    out_shape = (freqs, 2 * virtual, cols_here * width)
    dma = pltpu.SemaphoreType.DMA
    tile_buffer = pltpu.VMEM((3, tile_size, blocks, block, lines, share), jnp.bfloat16)
    freq_buffer = pltpu.VMEM((4, cols_here, blocks, block, 2 * virtual, width), jnp.bfloat16)
    wide = pltpu.VMEM((width // 128, 2 * F * virtual, 128), jnp.float32)
    estimate = pl.pallas_call(
        whole_kernel,
        out_shape=jax.ShapeDtypeStruct(out_shape, jnp.float32),
        grid=(steps,),
        in_specs=[smem(), smem()]
        + [vmem()] * 4
        + [
            spec(left_factor, left_index),
            spec(recorded, left_index),
            spec(weights_left, left_index),
            spec(right_factor, project_index),
            spec(weights_right, project_index),
            spec(right_factor, spread_index),
        ],
        out_specs=pl.BlockSpec((block,) + out_shape[1:], lambda s: (out_index(s), 0, 0)),
        scratch_shapes=[
            tile_buffer,
            tile_buffer,
            freq_buffer,
            freq_buffer,
            dma((3, blocks, tile_size)),
            dma((3, blocks, tile_size)),
            dma((4, blocks, cols_here)),
            dma((4, blocks, cols_here)),
            pltpu.VMEM((virtual, 2 * F, width), jnp.float32),
            wide,
            wide,
        ],
        compiler_params=pltpu.CompilerParams(
            vmem_limit_bytes=56 << 20,
            dimension_semantics=("arbitrary",),
            collective_id=0,
            has_side_effects=True,
        ),
    )(
        thresholds, step_sizes, *table_parts(), left_factor, recorded, weights_left,
        right_factor, weights_right, right_factor,
    )
    return estimate.reshape(freqs, 2, virtual, cols_here * width)


def either(*arrays):
    left_factor, right_factor = arrays[:2]
    cols_here = right_factor.shape[2]
    rank, width = left_factor.shape[4:]
    aligned = (
        cols_here == lax.axis_size("freq")
        and width % 128 == 0
        and 128 % (2 * rank) == 0
        and (cols_here * 2 * rank) % 128 == 0
        and arrays[4].shape[2] == 8
        and left_factor.shape[0] * lax.axis_size("freq") == F
    )
    return (per_device if aligned else per_device_plain)(*arrays)


def solution(mesh):
    return jax.shard_map(
        either,
        mesh=mesh,
        in_specs=(
            P("freq", "tile", None, None, None, None),
            P("freq", None, "tile", None, None, None),
            P("freq", None, None),
            P("freq", None, None, None),
            P("freq", None, None, "tile"),
            P("freq"),
            P(),
        ),
        out_specs=P("freq", None, None, "tile"),
        check_vma=False,
    )
```

```python
import functools
import math

import jax
import jax.numpy as jnp
import numpy as np
from jax import lax
from jax.experimental import pallas as pl
from jax.experimental.pallas import tpu as pltpu
from jax.sharding import PartitionSpec as P

F = 128


def dft_tables(freq_index, time_count):
    times_row = jnp.arange(time_count, dtype=jnp.int32)
    phase_steps = (freq_index[:, None] * times_row[None, :] % time_count).astype(jnp.float32)
    angles = phase_steps * (2.0 * math.pi / time_count)
    scaling = jnp.where(
        freq_index == 0, math.sqrt(1.0 / time_count), math.sqrt(2.0 / time_count)
    ).astype(jnp.float32)
    return (scaling[:, None] * jnp.cos(angles), scaling[:, None] * jnp.sin(angles))


def slot_weights(tile_ranks, tile_scales, rank_max):
    slot_index = jnp.arange(rank_max, dtype=jnp.int32)
    live_slots = (slot_index < tile_ranks[..., None]).astype(jnp.float32)
    return (tile_scales[:, 0] * tile_scales[:, 1])[..., None] * live_slots


def per_device_plain(
    left_factor, right_factor, tile_ranks, tile_scales, recorded, step_sizes, thresholds
):
    freqs_here = left_factor.shape[0]
    rows_here = left_factor.shape[1]
    col_tiles = left_factor.shape[2]
    rank_max = left_factor.shape[4]
    tile_width = left_factor.shape[5]
    row_tiles = right_factor.shape[1]
    cols_here = right_factor.shape[2]
    virtual = recorded.shape[2]
    tile_pos = lax.axis_index("tile")
    columns_here = cols_here * tile_width
    time_count = 2 * F
    highest = lax.Precision.HIGHEST
    weights = slot_weights(tile_ranks, tile_scales, rank_max)
    weights_right = lax.dynamic_slice_in_dim(weights, tile_pos * cols_here, cols_here, 2)
    weights_left = lax.dynamic_slice_in_dim(weights, tile_pos * rows_here, rows_here, 1)
    left_real = left_factor[:, :, :, 0]
    left_imag = left_factor[:, :, :, 1]
    right_real = right_factor[:, :, :, 0]
    right_imag = right_factor[:, :, :, 1]
    cos_all, sin_all = dft_tables(jnp.arange(F, dtype=jnp.int32), time_count)

    def gradient(residual):
        halves = residual.astype(jnp.bfloat16).reshape(
            freqs_here, 2, virtual, rows_here, tile_width
        )

        def contract_left(matrix, vectors):
            return jnp.einsum(
                "fijkq,fviq->fijkv", matrix, vectors, preferred_element_type=jnp.float32
            )

        dual_real = contract_left(left_real, halves[:, 0]) + contract_left(left_imag, halves[:, 1])
        dual_imag = contract_left(left_real, halves[:, 1]) - contract_left(left_imag, halves[:, 0])
        duals = (
            jnp.stack([dual_real, dual_imag], 3) * weights_left[:, :, :, None, :, None]
        ).astype(jnp.bfloat16)
        duals = duals.reshape(freqs_here, rows_here, col_tiles, 2, rank_max * virtual)
        arrived = lax.all_to_all(duals, "tile", split_axis=2, concat_axis=1, tiled=True)
        arrived = arrived.reshape(freqs_here, row_tiles, cols_here, 2, rank_max, virtual)

        def spread(matrix, vectors):
            return jnp.einsum(
                "fijkp,fijkv->fvjp", matrix, vectors, preferred_element_type=jnp.float32
            )

        grad_real = spread(right_real, arrived[:, :, :, 0]) - spread(
            right_imag, arrived[:, :, :, 1]
        )
        grad_imag = spread(right_real, arrived[:, :, :, 1]) + spread(
            right_imag, arrived[:, :, :, 0]
        )
        return jnp.stack([grad_real, grad_imag], 1).reshape(freqs_here, 2, virtual, columns_here)

    def to_time(wavefield):
        swapped = lax.all_to_all(wavefield, "freq", split_axis=3, concat_axis=0, tiled=True)
        return jnp.einsum("fvn,ft->nvt", swapped[:, 0], cos_all, precision=highest) - jnp.einsum(
            "fvn,ft->nvt", swapped[:, 1], sin_all, precision=highest
        )

    def shrink(signal):
        excess = jnp.abs(signal) - thresholds[None, :, None]
        return jnp.sign(signal) * jnp.maximum(excess, 0.0)

    def to_freq(signal):
        real_part = jnp.einsum("nvt,ft->fvn", signal, cos_all, precision=highest)
        imag_part = -jnp.einsum("nvt,ft->fvn", signal, sin_all, precision=highest)
        return lax.all_to_all(
            jnp.stack([real_part, imag_part], 1), "freq", split_axis=0, concat_axis=3, tiled=True
        )

    scaled = step_sizes[:, None, None, None]
    first = to_freq(shrink(to_time(scaled * gradient(recorded))))
    halves = first.astype(jnp.bfloat16).reshape(freqs_here, 2, virtual, cols_here, tile_width)

    def project(matrix, vectors):
        return jnp.einsum("fijkp,fvjp->fijkv", matrix, vectors, preferred_element_type=jnp.float32)

    coef_real = project(right_real, halves[:, 0]) + project(right_imag, halves[:, 1])
    coef_imag = project(right_real, halves[:, 1]) - project(right_imag, halves[:, 0])
    coeffs = (jnp.stack([coef_real, coef_imag], 3) * weights_right[:, :, :, None, :, None]).astype(
        jnp.bfloat16
    )
    coeffs = coeffs.reshape(freqs_here, row_tiles, cols_here, 2, rank_max * virtual)
    arrived = lax.all_to_all(coeffs, "tile", split_axis=1, concat_axis=2, tiled=True)
    arrived = arrived.reshape(freqs_here, rows_here, col_tiles, 2, rank_max, virtual)

    def expand(matrix, vectors):
        return jnp.einsum("fijkq,fijkv->fviq", matrix, vectors, preferred_element_type=jnp.float32)

    image_real = expand(left_real, arrived[:, :, :, 0]) - expand(left_imag, arrived[:, :, :, 1])
    image_imag = expand(left_real, arrived[:, :, :, 1]) + expand(left_imag, arrived[:, :, :, 0])
    return to_freq(
        shrink(
            to_time(
                first
                + scaled
                * gradient(
                    recorded
                    - jnp.stack([image_real, image_imag], 1).reshape(
                        freqs_here, 2, virtual, rows_here * tile_width
                    )
                )
            )
        )
    )


def swap_parts(values, first_part, half):
    pieces = []
    for start in range(0, values.shape[1], 128):
        piece = values[:, start : start + 128]
        pieces.append(
            jnp.where(
                first_part, pltpu.roll(piece, 128 - half, 1), pltpu.roll(piece, half, 1)
            )
        )
    return jnp.concatenate(pieces, 1)


def lane_ids(rows, lanes):
    return lax.broadcasted_iota(jnp.int32, (rows, lanes), 1)


def adjoint_rows(product, half):
    virtual = product.shape[0] // 2
    lanes = product.shape[1]
    sign = jnp.where(lane_ids(virtual, lanes) // half % 2 == 0, 1.0, -1.0)
    first_part = lane_ids(virtual, 128) // half % 2 == 0
    return product[:virtual] * sign + swap_parts(product[virtual:], first_part, half)


def forward_rows(coefs, half):
    rows, lanes = coefs.shape
    sign = jnp.where(lane_ids(rows, lanes) // half % 2 == 0, 1.0, -1.0)
    first_part = lane_ids(rows, 128) // half % 2 == 0
    return coefs * sign, swap_parts(coefs, first_part, half)


def nt_dot(a, b):
    return lax.dot_general(a, b, (((1,), (1,)), ((), ())), preferred_element_type=jnp.float32)


def nn_dot(a, b):
    return jnp.dot(a, b, preferred_element_type=jnp.float32)


def dual_of(left_rows, field, weight, half):
    return adjoint_rows(nt_dot(field.astype(jnp.bfloat16), left_rows), half) * weight


def store_duals(out_ref, at, duals, peers):
    together = jnp.concatenate(duals, 0)
    width = together.shape[1] // peers
    for peer in range(peers):
        out_ref[peer, at] = together[:, peer * width : (peer + 1) * width].astype(jnp.bfloat16)


def dual_kernel(base, left_ref, recorded_ref, weight_ref, out_ref):
    freqs, rows, cols, _, rank, width = left_ref.shape
    peers = out_ref.shape[0]
    for at in range(freqs):
        duals = []
        for row in range(rows):
            left_rows = left_ref[at, row].reshape(cols * 2 * rank, width)
            part = recorded_ref[at, :, :, row * width : (row + 1) * width]
            field = part.reshape(-1, width)
            duals.append(dual_of(left_rows, field, weight_ref[pl.ds((base + at) * rows + row, 1), :], rank))
        store_duals(out_ref, at, duals, peers)


def image_kernel(base, left_ref, coefs_ref, recorded_ref, weight_ref, out_ref):
    freqs, rows, cols, _, rank, width = left_ref.shape
    peers = coefs_ref.shape[0]
    share = cols // peers * 2 * rank
    virtual = recorded_ref.shape[2]
    for at in range(freqs):
        forms = [
            forward_rows(coefs_ref[peer, at].astype(jnp.float32), rank) for peer in range(peers)
        ]
        duals = []
        for row in range(rows):
            left_rows = left_ref[at, row].reshape(cols * 2 * rank, width)
            own = slice(row * virtual, (row + 1) * virtual)
            image = 0.0
            for peer, (real_form, imag_form) in enumerate(forms):
                both = jnp.concatenate([real_form[own], imag_form[own]], 0).astype(jnp.bfloat16)
                image += nn_dot(both, left_rows[peer * share : (peer + 1) * share])
            part = recorded_ref[at, :, :, row * width : (row + 1) * width]
            field = part.reshape(-1, width) - image
            duals.append(dual_of(left_rows, field, weight_ref[pl.ds((base + at) * rows + row, 1), :], rank))
        store_duals(out_ref, at, duals, peers)


def spread_kernel(base, steps_ref, right_ref, duals_ref, out_ref):
    freqs, rows, cols, _, rank, width = right_ref.shape
    peers, _, both, share = duals_ref.shape
    rows_each = rows // peers
    virtual = both // rows_each
    group = 2 * rank
    owner = lane_ids(2 * virtual, share) // group
    for at in range(freqs):
        wide = []
        for peer in range(peers):
            real_form, imag_form = forward_rows(duals_ref[peer, at].astype(jnp.float32), rank)
            for row in range(rows_each):
                own = slice(row * virtual, (row + 1) * virtual)
                rows_both = jnp.concatenate([real_form[own], imag_form[own]], 0)
                wide.append(
                    jnp.concatenate(
                        [jnp.where(owner == col, rows_both, 0.0) for col in range(cols)], 0
                    ).astype(jnp.bfloat16)
                )
        total = 0.0
        for row in range(rows):
            total += nn_dot(wide[row], right_ref[at, row].reshape(cols * group, width))
        step = steps_ref[base + at]
        out_ref[:, at] = (total * step).astype(jnp.bfloat16).reshape(cols, 2 * virtual, width)


def project_kernel(base, right_ref, field_ref, weight_ref, out_ref):
    freqs, rows, cols, _, rank, width = right_ref.shape
    peers, _, both, share = out_ref.shape
    rows_each = rows // peers
    virtual = both // rows_each
    group = 2 * rank
    owner = lane_ids(2 * virtual, 128) // group
    per_piece = 128 // group
    for at in range(freqs):
        field = field_ref[:, at].reshape(cols * 2 * virtual, width)
        for peer in range(peers):
            coefs = []
            for row in range(peer * rows_each, (peer + 1) * rows_each):
                product = nt_dot(field, right_ref[at, row].reshape(cols * group, width))
                pieces = []
                for start in range(0, share, 128):
                    piece = 0.0
                    for step in range(per_piece):
                        col = start // group + step
                        rows_of = product[
                            col * 2 * virtual : (col + 1) * 2 * virtual, start : start + 128
                        ]
                        piece = rows_of if step == 0 else jnp.where(owner == step, rows_of, piece)
                    pieces.append(piece)
                picked = jnp.concatenate(pieces, 1)
                weight = weight_ref[pl.ds((base + at) * rows + row, 1), :]
                coefs.append(adjoint_rows(picked, rank) * weight)
            out_ref[peer, at] = jnp.concatenate(coefs, 0).astype(jnp.bfloat16)


def split_two(values):
    high = values.astype(jnp.bfloat16)
    return high, (values - high.astype(jnp.float32)).astype(jnp.bfloat16)


def shrink_kernel(second, levels_ref, tables, field_ref, kept_ref, out_ref, wide, packed):
    to_high, to_low, back_high, back_low = tables
    virtual = levels_ref.shape[0]
    width = field_ref.shape[-1]
    times, lines = to_high.shape
    halves = [slice(at, at + 128) for at in range(0, width, 128)]
    for half, lanes in enumerate(halves):
        wide[half] = (
            field_ref[:, :, :, :, lanes].astype(jnp.float32).reshape(lines * virtual, 128)
        )
    odd = lax.broadcasted_iota(jnp.int32, (times, width), 0) % 2
    turn = jnp.where(odd == 0, 1.0, -1.0)
    for source in range(virtual):
        own = pl.ds(source, lines, stride=virtual)
        spectrum = jnp.concatenate(
            [wide[half, own, :] for half in range(len(halves))], 1
        ).astype(jnp.bfloat16)
        signal = nn_dot(to_high[...], spectrum) + nn_dot(to_low[...], spectrum)
        if second:
            signal += kept_ref[source]
        level = levels_ref[source]
        shrunk = signal - jnp.minimum(jnp.maximum(signal, -level), level)
        if not second:
            mean = jnp.sum(shrunk * turn, 0, keepdims=True) * (1.0 / times)
            kept_ref[source] = shrunk - turn * mean
        high, low = split_two(shrunk)
        freq = nn_dot(back_high[...], high) + nn_dot(back_low[...], high) + nn_dot(
            back_high[...], low
        )
        for half, lanes in enumerate(halves):
            packed[half, own, :] = freq[:, lanes]
    for half, lanes in enumerate(halves):
        out_ref[:, :, :, :, lanes] = (
            packed[half].astype(jnp.bfloat16).reshape(out_ref.shape[:-1] + (128,))
        )


class Exchange:
    def __init__(self, axis, send, recv, send_sem, recv_sem):
        self.axis, self.send, self.recv = axis, send, recv
        self.send_sem, self.recv_sem = send_sem, recv_sem
        self.size = send.shape[0]
        self.me = lax.axis_index(axis)

    def peers(self):
        return [lax.rem(self.me + step, self.size) for step in range(1, self.size)]

    def copy(self, block, peer, source):
        return pltpu.make_async_remote_copy(
            src_ref=self.send.at[peer, block],
            dst_ref=self.recv.at[source, block],
            send_sem=self.send_sem.at[block, peer],
            recv_sem=self.recv_sem.at[block, source],
            device_id={self.axis: peer},
            device_id_type=pl.DeviceIdType.MESH,
        )

    def start(self, block):
        for peer in self.peers():
            self.copy(block, peer, self.me).start()
        self.recv[self.me, block] = self.send[self.me, block]

    def start_all(self):
        @pl.loop(0, self.send.shape[1])
        def _(block):
            self.start(block)

    def wait(self, block):
        for peer in self.peers():
            self.copy(block, peer, peer).wait_recv()

    def wait_all(self):
        @pl.loop(0, self.send.shape[1])
        def _(block):
            self.wait(block)

    def finish(self):
        @pl.loop(0, self.send.shape[1])
        def _(block):
            for peer in self.peers():
                self.copy(block, peer, self.me).wait_send()


def stages(blocks):
    lag = LAG
    first_shrink = blocks + lag
    second_shrink = first_shrink + blocks + 2 * lag
    return lag, first_shrink, second_shrink, second_shrink + blocks


def whole_kernel(
    levels_ref, steps_ref, to_high, to_low, back_high, back_low,
    left_hbm, right_hbm, recorded_ref, cells_left_ref, cells_right_ref,
    out_ref,
    left, right, left_sem, right_sem, weight_left_ref, weight_right_ref,
    tile_send, tile_recv, freq_send, freq_recv, tile_ssem, tile_rsem, freq_ssem, freq_rsem,
    kept, wide, packed,
):
    step = pl.program_id(0)
    block = left.shape[1]
    rank = left.shape[5]
    blocks = tile_send.shape[2]
    lag, first_shrink, second_shrink, last = stages(blocks)
    tables = (to_high, to_low, back_high, back_low)
    over_tile = [
        Exchange("tile", tile_send.at[n], tile_recv.at[n], tile_ssem.at[n], tile_rsem.at[n])
        for n in range(tile_send.shape[0])
    ]
    over_freq = [
        Exchange("freq", freq_send.at[n], freq_recv.at[n], freq_ssem.at[n], freq_rsem.at[n])
        for n in range(freq_send.shape[0])
    ]

    def span(start):
        return (step >= start) & (step < start + blocks)

    def fetch(source, target, sem, at):
        return pltpu.make_async_copy(
            source.at[pl.ds(at * block, block)], target.at[at], sem.at[at]
        )

    def fetch_both(at):
        fetch(left_hbm, left, left_sem, at).start()
        fetch(right_hbm, right, right_sem, at).start()

    @pl.when(step == 0)
    def _():
        for at in range(min(AHEAD, blocks)):
            fetch_both(at)

    @pl.when(step + AHEAD < blocks)
    def _():
        fetch_both(step + AHEAD)

    @pl.when(step == 0)
    def _():
        barrier = pltpu.get_barrier_semaphore()
        count = 0
        for exchange in (over_tile[0], over_freq[0]):
            for peer in exchange.peers():
                pl.semaphore_signal(
                    barrier, inc=1, device_id={exchange.axis: peer},
                    device_id_type=pl.DeviceIdType.MESH,
                )
                count += 1
        lane_weights(cells_left_ref, weight_left_ref, rank)
        lane_weights(cells_right_ref, weight_right_ref, rank)
        pl.semaphore_wait(barrier, count)

    @pl.when(span(0))
    def _():
        fetch(left_hbm, left, left_sem, step).wait()
        dual_kernel(
            step * block, left.at[step], recorded_ref, weight_left_ref,
            over_tile[0].send.at[:, step],
        )
        over_tile[0].start(step)

    def spread(start, tiles, freqs):
        @pl.when(span(start))
        def _():
            b = step - start
            if start == lag:
                fetch(right_hbm, right, right_sem, b).wait()
            tiles.wait(b)
            spread_kernel(
                b * block, steps_ref, right.at[b], tiles.recv.at[:, b], freqs.send.at[:, b]
            )
            freqs.start(b)

    spread(lag, over_tile[0], over_freq[0])

    @pl.when(step == first_shrink)
    def _():
        over_freq[0].wait_all()
        shrink_kernel(
            False, levels_ref, tables, over_freq[0].recv, kept, over_freq[1].send, wide, packed
        )
        over_freq[1].start_all()

    @pl.when(span(first_shrink))
    def _():
        b = step - first_shrink
        over_freq[1].wait(b)
        project_kernel(
            b * block, right.at[b], over_freq[1].recv.at[:, b], weight_right_ref,
            over_tile[1].send.at[:, b],
        )
        over_tile[1].start(b)

    @pl.when(span(first_shrink + lag))
    def _():
        b = step - first_shrink - lag
        over_tile[1].wait(b)
        image_kernel(
            b * block, left.at[b], over_tile[1].recv.at[:, b], recorded_ref, weight_left_ref,
            over_tile[2].send.at[:, b],
        )
        over_tile[2].start(b)

    spread(first_shrink + 2 * lag, over_tile[2], over_freq[2])

    @pl.when(step == second_shrink)
    def _():
        over_freq[2].wait_all()
        shrink_kernel(
            True, levels_ref, tables, over_freq[2].recv, kept, over_freq[3].send, wide, packed
        )
        over_freq[3].start_all()

    @pl.when(span(second_shrink))
    def _():
        b = step - second_shrink
        over_freq[3].wait(b)
        peers, _, at_once, rows, width = over_freq[3].recv.shape
        for at in range(at_once):
            for peer in range(peers):
                out_ref[at, :, peer * width : (peer + 1) * width] = over_freq[3].recv[
                    peer, b, at
                ]

    @pl.when(step == last - 1)
    def _():
        for exchange in over_tile + over_freq:
            exchange.finish()


LAG = 2
AHEAD = 3


def lane_weights(cells_ref, out_ref, rank):
    _, rows, tiles = cells_ref.shape
    lanes = out_ref.shape[1]
    owner = lax.broadcasted_iota(jnp.int32, (tiles, lanes), 1) // (2 * rank)
    pick = (owner == lax.broadcasted_iota(jnp.int32, (tiles, lanes), 0)).astype(jnp.float32)
    widen = lambda values: jnp.dot(
        values, pick, precision=lax.Precision.HIGHEST, preferred_element_type=jnp.float32
    )
    slot = (lane_ids(rows, lanes) % rank).astype(jnp.float32)
    out_ref[...] = jnp.where(slot < widen(cells_ref[0]) - 0.5, widen(cells_ref[1]), 0.0)


def table_parts():
    times = 2 * F
    freq = np.arange(F)[:, None]
    angles = (freq * np.arange(times)[None, :] % times) * (2.0 * math.pi / times)
    scaling = np.where(freq == 0, math.sqrt(1.0 / times), math.sqrt(2.0 / times))
    table = np.stack([scaling * np.cos(angles), -scaling * np.sin(angles)], 1)
    table = table.reshape(2 * F, times).astype(np.float32)
    high = table.astype(jnp.bfloat16)
    low = (table - high.astype(np.float32)).astype(jnp.bfloat16)
    return tuple(jnp.asarray(part) for part in (high.T, low.T, high, low))


def vmem():
    return pl.BlockSpec(memory_space=pltpu.VMEM)


def smem():
    return pl.BlockSpec(memory_space=pltpu.SMEM)


def per_device(
    left_factor, right_factor, tile_ranks, tile_scales, recorded, step_sizes, thresholds
):
    freqs, rows_here, col_tiles, _, rank, width = left_factor.shape
    row_tiles, cols_here = right_factor.shape[1:3]
    virtual = recorded.shape[2]
    tile_size = col_tiles // cols_here
    share = cols_here * 2 * rank
    lines = rows_here * virtual
    tile_pos = lax.axis_index("tile")
    block = 2 if freqs % 2 == 0 else 1
    blocks = freqs // block
    lag, first_shrink, second_shrink, steps = stages(blocks)

    cells = jnp.stack(
        [tile_ranks.astype(jnp.float32), tile_scales[:, 0] * tile_scales[:, 1]]
    )
    cells_left = lax.dynamic_slice_in_dim(cells, tile_pos * rows_here, rows_here, 2)
    cells_left = cells_left.reshape(2, freqs * rows_here, col_tiles)
    cells_right = lax.dynamic_slice_in_dim(cells, tile_pos * cols_here, cols_here, 3)
    cells_right = cells_right.reshape(2, freqs * row_tiles, cols_here)

    def spec(array, index):
        rest = array.shape[1:]
        return pl.BlockSpec((block,) + rest, lambda s: (index(s),) + (0,) * len(rest))

    def within(at):
        return jnp.minimum(jnp.maximum(at, 0), blocks - 1)

    def left_index(s):
        return jnp.where(s < blocks, s, within(s - first_shrink - lag))

    def out_index(s):
        return within(s - second_shrink)

    out_shape = (freqs, 2 * virtual, cols_here * width)
    dma = pltpu.SemaphoreType.DMA
    tile_buffer = pltpu.VMEM((3, tile_size, blocks, block, lines, share), jnp.bfloat16)
    freq_buffer = pltpu.VMEM((4, cols_here, blocks, block, 2 * virtual, width), jnp.bfloat16)
    wide = pltpu.VMEM((width // 128, 2 * F * virtual, 128), jnp.float32)
    estimate = pl.pallas_call(
        whole_kernel,
        out_shape=jax.ShapeDtypeStruct(out_shape, jnp.bfloat16),
        grid=(steps,),
        in_specs=[smem(), smem()]
        + [vmem()] * 4
        + [pl.BlockSpec(memory_space=pl.ANY)] * 2
        + [spec(recorded, left_index), vmem(), vmem()],
        out_specs=pl.BlockSpec((block,) + out_shape[1:], lambda s: (out_index(s), 0, 0)),
        scratch_shapes=[
            pltpu.VMEM((blocks, block) + left_factor.shape[1:], jnp.bfloat16),
            pltpu.VMEM((blocks, block) + right_factor.shape[1:], jnp.bfloat16),
            dma((blocks,)),
            dma((blocks,)),
            pltpu.VMEM((freqs * rows_here, col_tiles * 2 * rank), jnp.float32),
            pltpu.VMEM((freqs * row_tiles, share), jnp.float32),
            tile_buffer,
            tile_buffer,
            freq_buffer,
            freq_buffer,
            dma((3, blocks, tile_size)),
            dma((3, blocks, tile_size)),
            dma((4, blocks, cols_here)),
            dma((4, blocks, cols_here)),
            pltpu.VMEM((virtual, 2 * F, width), jnp.float32),
            wide,
            wide,
        ],
        compiler_params=pltpu.CompilerParams(
            vmem_limit_bytes=58 << 20,
            dimension_semantics=("arbitrary",),
            collective_id=0,
            has_side_effects=True,
        ),
    )(
        thresholds, step_sizes, *table_parts(), left_factor, right_factor, recorded,
        cells_left, cells_right,
    )
    return estimate.astype(jnp.float32).reshape(freqs, 2, virtual, cols_here * width)


def either(*arrays):
    left_factor, right_factor = arrays[:2]
    cols_here = right_factor.shape[2]
    rank, width = left_factor.shape[4:]
    aligned = (
        cols_here == lax.axis_size("freq")
        and width % 128 == 0
        and 128 % (2 * rank) == 0
        and (cols_here * 2 * rank) % 128 == 0
        and arrays[4].shape[2] == 8
        and left_factor.shape[0] * lax.axis_size("freq") == F
    )
    return (per_device if aligned else per_device_plain)(*arrays)


def solution(mesh):
    return jax.shard_map(
        either,
        mesh=mesh,
        in_specs=(
            P("freq", "tile", None, None, None, None),
            P("freq", None, "tile", None, None, None),
            P("freq", None, None),
            P("freq", None, None, None),
            P("freq", None, None, "tile"),
            P("freq"),
            P(),
        ),
        out_specs=P("freq", None, None, "tile"),
        check_vma=False,
    )
```

```python
import functools
import math

import jax
import jax.numpy as jnp
import numpy as np
from jax import lax
from jax.experimental import pallas as pl
from jax.experimental.pallas import tpu as pltpu
from jax.sharding import PartitionSpec as P

F = 128


def dft_tables(freq_index, time_count):
    times_row = jnp.arange(time_count, dtype=jnp.int32)
    phase_steps = (freq_index[:, None] * times_row[None, :] % time_count).astype(jnp.float32)
    angles = phase_steps * (2.0 * math.pi / time_count)
    scaling = jnp.where(
        freq_index == 0, math.sqrt(1.0 / time_count), math.sqrt(2.0 / time_count)
    ).astype(jnp.float32)
    return (scaling[:, None] * jnp.cos(angles), scaling[:, None] * jnp.sin(angles))


def slot_weights(tile_ranks, tile_scales, rank_max):
    slot_index = jnp.arange(rank_max, dtype=jnp.int32)
    live_slots = (slot_index < tile_ranks[..., None]).astype(jnp.float32)
    return (tile_scales[:, 0] * tile_scales[:, 1])[..., None] * live_slots


def per_device_plain(
    left_factor, right_factor, tile_ranks, tile_scales, recorded, step_sizes, thresholds
):
    freqs_here = left_factor.shape[0]
    rows_here = left_factor.shape[1]
    col_tiles = left_factor.shape[2]
    rank_max = left_factor.shape[4]
    tile_width = left_factor.shape[5]
    row_tiles = right_factor.shape[1]
    cols_here = right_factor.shape[2]
    virtual = recorded.shape[2]
    tile_pos = lax.axis_index("tile")
    columns_here = cols_here * tile_width
    time_count = 2 * F
    highest = lax.Precision.HIGHEST
    weights = slot_weights(tile_ranks, tile_scales, rank_max)
    weights_right = lax.dynamic_slice_in_dim(weights, tile_pos * cols_here, cols_here, 2)
    weights_left = lax.dynamic_slice_in_dim(weights, tile_pos * rows_here, rows_here, 1)
    left_real = left_factor[:, :, :, 0]
    left_imag = left_factor[:, :, :, 1]
    right_real = right_factor[:, :, :, 0]
    right_imag = right_factor[:, :, :, 1]
    cos_all, sin_all = dft_tables(jnp.arange(F, dtype=jnp.int32), time_count)

    def gradient(residual):
        halves = residual.astype(jnp.bfloat16).reshape(
            freqs_here, 2, virtual, rows_here, tile_width
        )

        def contract_left(matrix, vectors):
            return jnp.einsum(
                "fijkq,fviq->fijkv", matrix, vectors, preferred_element_type=jnp.float32
            )

        dual_real = contract_left(left_real, halves[:, 0]) + contract_left(left_imag, halves[:, 1])
        dual_imag = contract_left(left_real, halves[:, 1]) - contract_left(left_imag, halves[:, 0])
        duals = (
            jnp.stack([dual_real, dual_imag], 3) * weights_left[:, :, :, None, :, None]
        ).astype(jnp.bfloat16)
        duals = duals.reshape(freqs_here, rows_here, col_tiles, 2, rank_max * virtual)
        arrived = lax.all_to_all(duals, "tile", split_axis=2, concat_axis=1, tiled=True)
        arrived = arrived.reshape(freqs_here, row_tiles, cols_here, 2, rank_max, virtual)

        def spread(matrix, vectors):
            return jnp.einsum(
                "fijkp,fijkv->fvjp", matrix, vectors, preferred_element_type=jnp.float32
            )

        grad_real = spread(right_real, arrived[:, :, :, 0]) - spread(
            right_imag, arrived[:, :, :, 1]
        )
        grad_imag = spread(right_real, arrived[:, :, :, 1]) + spread(
            right_imag, arrived[:, :, :, 0]
        )
        return jnp.stack([grad_real, grad_imag], 1).reshape(freqs_here, 2, virtual, columns_here)

    def to_time(wavefield):
        swapped = lax.all_to_all(wavefield, "freq", split_axis=3, concat_axis=0, tiled=True)
        return jnp.einsum("fvn,ft->nvt", swapped[:, 0], cos_all, precision=highest) - jnp.einsum(
            "fvn,ft->nvt", swapped[:, 1], sin_all, precision=highest
        )

    def shrink(signal):
        excess = jnp.abs(signal) - thresholds[None, :, None]
        return jnp.sign(signal) * jnp.maximum(excess, 0.0)

    def to_freq(signal):
        real_part = jnp.einsum("nvt,ft->fvn", signal, cos_all, precision=highest)
        imag_part = -jnp.einsum("nvt,ft->fvn", signal, sin_all, precision=highest)
        return lax.all_to_all(
            jnp.stack([real_part, imag_part], 1), "freq", split_axis=0, concat_axis=3, tiled=True
        )

    scaled = step_sizes[:, None, None, None]
    first = to_freq(shrink(to_time(scaled * gradient(recorded))))
    halves = first.astype(jnp.bfloat16).reshape(freqs_here, 2, virtual, cols_here, tile_width)

    def project(matrix, vectors):
        return jnp.einsum("fijkp,fvjp->fijkv", matrix, vectors, preferred_element_type=jnp.float32)

    coef_real = project(right_real, halves[:, 0]) + project(right_imag, halves[:, 1])
    coef_imag = project(right_real, halves[:, 1]) - project(right_imag, halves[:, 0])
    coeffs = (jnp.stack([coef_real, coef_imag], 3) * weights_right[:, :, :, None, :, None]).astype(
        jnp.bfloat16
    )
    coeffs = coeffs.reshape(freqs_here, row_tiles, cols_here, 2, rank_max * virtual)
    arrived = lax.all_to_all(coeffs, "tile", split_axis=1, concat_axis=2, tiled=True)
    arrived = arrived.reshape(freqs_here, rows_here, col_tiles, 2, rank_max, virtual)

    def expand(matrix, vectors):
        return jnp.einsum("fijkq,fijkv->fviq", matrix, vectors, preferred_element_type=jnp.float32)

    image_real = expand(left_real, arrived[:, :, :, 0]) - expand(left_imag, arrived[:, :, :, 1])
    image_imag = expand(left_real, arrived[:, :, :, 1]) + expand(left_imag, arrived[:, :, :, 0])
    return to_freq(
        shrink(
            to_time(
                first
                + scaled
                * gradient(
                    recorded
                    - jnp.stack([image_real, image_imag], 1).reshape(
                        freqs_here, 2, virtual, rows_here * tile_width
                    )
                )
            )
        )
    )


def swap_parts(values, first_part, half):
    pieces = []
    for start in range(0, values.shape[1], 128):
        piece = values[:, start : start + 128]
        pieces.append(
            jnp.where(
                first_part, pltpu.roll(piece, 128 - half, 1), pltpu.roll(piece, half, 1)
            )
        )
    return jnp.concatenate(pieces, 1)


def lane_ids(rows, lanes):
    return lax.broadcasted_iota(jnp.int32, (rows, lanes), 1)


def adjoint_rows(product, half):
    virtual = product.shape[0] // 2
    lanes = product.shape[1]
    sign = jnp.where(lane_ids(virtual, lanes) // half % 2 == 0, 1.0, -1.0)
    first_part = lane_ids(virtual, 128) // half % 2 == 0
    return product[:virtual] * sign + swap_parts(product[virtual:], first_part, half)


def forward_rows(coefs, half):
    rows, lanes = coefs.shape
    sign = jnp.where(lane_ids(rows, lanes) // half % 2 == 0, 1.0, -1.0)
    first_part = lane_ids(rows, 128) // half % 2 == 0
    return coefs * sign, swap_parts(coefs, first_part, half)


def nt_dot(a, b):
    return lax.dot_general(a, b, (((1,), (1,)), ((), ())), preferred_element_type=jnp.float32)


def nn_dot(a, b):
    return jnp.dot(a, b, preferred_element_type=jnp.float32)


def dual_of(left_rows, field, weight, half):
    return adjoint_rows(nt_dot(field.astype(jnp.bfloat16), left_rows), half) * weight


def store_duals(out_ref, at, duals, peers):
    together = jnp.concatenate(duals, 0)
    width = together.shape[1] // peers
    for peer in range(peers):
        out_ref[peer, at] = together[:, peer * width : (peer + 1) * width].astype(jnp.bfloat16)


def dual_kernel(base, all_rows, left_ref, recorded_ref, weight_ref, out_ref):
    freqs, rows, cols, _, rank, width = left_ref.shape
    peers = out_ref.shape[0]
    for at in range(freqs):
        duals = []
        for row in range(rows):
            left_rows = left_ref[at, row].reshape(cols * 2 * rank, width)
            part = recorded_ref[at, :, :, row * width : (row + 1) * width]
            field = part.reshape(-1, width)
            duals.append(dual_of(left_rows, field, weight_ref[pl.ds(base + at * all_rows + row, 1), :], rank))
        store_duals(out_ref, at, duals, peers)


def image_kernel(base, all_rows, left_ref, coefs_ref, recorded_ref, weight_ref, out_ref):
    freqs, rows, cols, _, rank, width = left_ref.shape
    peers = coefs_ref.shape[0]
    share = cols // peers * 2 * rank
    virtual = recorded_ref.shape[2]
    for at in range(freqs):
        forms = [
            forward_rows(coefs_ref[peer, at].astype(jnp.float32), rank) for peer in range(peers)
        ]
        duals = []
        for row in range(rows):
            left_rows = left_ref[at, row].reshape(cols * 2 * rank, width)
            own = slice(row * virtual, (row + 1) * virtual)
            image = 0.0
            for peer, (real_form, imag_form) in enumerate(forms):
                both = jnp.concatenate([real_form[own], imag_form[own]], 0).astype(jnp.bfloat16)
                image += nn_dot(both, left_rows[peer * share : (peer + 1) * share])
            part = recorded_ref[at, :, :, row * width : (row + 1) * width]
            field = part.reshape(-1, width) - image
            duals.append(dual_of(left_rows, field, weight_ref[pl.ds(base + at * all_rows + row, 1), :], rank))
        store_duals(out_ref, at, duals, peers)


def spread_kernel(base, steps_ref, right_ref, duals_ref, out_ref):
    freqs, rows, cols, _, rank, width = right_ref.shape
    peers, _, both, share = duals_ref.shape
    rows_each = rows // peers
    virtual = both // rows_each
    group = 2 * rank
    owner = lane_ids(2 * virtual, share) // group
    for at in range(freqs):
        wide = []
        for peer in range(peers):
            real_form, imag_form = forward_rows(duals_ref[peer, at].astype(jnp.float32), rank)
            for row in range(rows_each):
                own = slice(row * virtual, (row + 1) * virtual)
                rows_both = jnp.concatenate([real_form[own], imag_form[own]], 0)
                wide.append(
                    jnp.concatenate(
                        [jnp.where(owner == col, rows_both, 0.0) for col in range(cols)], 0
                    ).astype(jnp.bfloat16)
                )
        total = 0.0
        for row in range(rows):
            total += nn_dot(wide[row], right_ref[at, row].reshape(cols * group, width))
        step = steps_ref[base + at]
        out_ref[:, at] = (total * step).astype(jnp.bfloat16).reshape(cols, 2 * virtual, width)


def project_kernel(base, right_ref, field_ref, weight_ref, out_ref):
    freqs, rows, cols, _, rank, width = right_ref.shape
    peers, _, both, share = out_ref.shape
    rows_each = rows // peers
    virtual = both // rows_each
    group = 2 * rank
    owner = lane_ids(2 * virtual, 128) // group
    per_piece = 128 // group
    for at in range(freqs):
        field = field_ref[:, at].reshape(cols * 2 * virtual, width)
        for peer in range(peers):
            coefs = []
            for row in range(peer * rows_each, (peer + 1) * rows_each):
                product = nt_dot(field, right_ref[at, row].reshape(cols * group, width))
                pieces = []
                for start in range(0, share, 128):
                    piece = 0.0
                    for step in range(per_piece):
                        col = start // group + step
                        rows_of = product[
                            col * 2 * virtual : (col + 1) * 2 * virtual, start : start + 128
                        ]
                        piece = rows_of if step == 0 else jnp.where(owner == step, rows_of, piece)
                    pieces.append(piece)
                picked = jnp.concatenate(pieces, 1)
                weight = weight_ref[pl.ds((base + at) * rows + row, 1), :]
                coefs.append(adjoint_rows(picked, rank) * weight)
            out_ref[peer, at] = jnp.concatenate(coefs, 0).astype(jnp.bfloat16)


def split_two(values):
    high = values.astype(jnp.bfloat16)
    return high, (values - high.astype(jnp.float32)).astype(jnp.bfloat16)


def shrink_kernel(second, levels_ref, tables, field_ref, kept_ref, out_ref, wide, packed):
    to_high, to_low, back_high, back_low = tables
    virtual = levels_ref.shape[0]
    width = field_ref.shape[-1]
    times, lines = to_high.shape
    halves = [slice(at, at + 128) for at in range(0, width, 128)]
    for half, lanes in enumerate(halves):
        wide[half] = (
            field_ref[:, :, :, :, lanes].astype(jnp.float32).reshape(lines * virtual, 128)
        )
    odd = lax.broadcasted_iota(jnp.int32, (times, width), 0) % 2
    turn = jnp.where(odd == 0, 1.0, -1.0)
    for source in range(virtual):
        own = pl.ds(source, lines, stride=virtual)
        spectrum = jnp.concatenate(
            [wide[half, own, :] for half in range(len(halves))], 1
        ).astype(jnp.bfloat16)
        signal = nn_dot(to_high[...], spectrum) + nn_dot(to_low[...], spectrum)
        if second:
            signal += kept_ref[source]
        level = levels_ref[source]
        shrunk = signal - jnp.minimum(jnp.maximum(signal, -level), level)
        if not second:
            mean = jnp.sum(shrunk * turn, 0, keepdims=True) * (1.0 / times)
            kept_ref[source] = shrunk - turn * mean
        high, low = split_two(shrunk)
        freq = nn_dot(back_high[...], high) + nn_dot(back_low[...], high) + nn_dot(
            back_high[...], low
        )
        for half, lanes in enumerate(halves):
            packed[half, own, :] = freq[:, lanes]
    for half, lanes in enumerate(halves):
        out_ref[:, :, :, :, lanes] = (
            packed[half].astype(jnp.bfloat16).reshape(out_ref.shape[:-1] + (128,))
        )


class Exchange:
    def __init__(self, axis, send, recv, send_sem, recv_sem):
        self.axis, self.send, self.recv = axis, send, recv
        self.send_sem, self.recv_sem = send_sem, recv_sem
        self.size = send.shape[0]
        self.me = lax.axis_index(axis)

    def peers(self):
        return [lax.rem(self.me + step, self.size) for step in range(1, self.size)]

    def copy(self, block, peer, source):
        return pltpu.make_async_remote_copy(
            src_ref=self.send.at[peer, block],
            dst_ref=self.recv.at[source, block],
            send_sem=self.send_sem.at[block, peer],
            recv_sem=self.recv_sem.at[block, source],
            device_id={self.axis: peer},
            device_id_type=pl.DeviceIdType.MESH,
        )

    def start(self, block):
        for peer in self.peers():
            self.copy(block, peer, self.me).start()
        self.recv[self.me, block] = self.send[self.me, block]

    def start_all(self):
        @pl.loop(0, self.send.shape[1])
        def _(block):
            self.start(block)

    def wait(self, block):
        for peer in self.peers():
            self.copy(block, peer, peer).wait_recv()

    def wait_all(self):
        @pl.loop(0, self.send.shape[1])
        def _(block):
            self.wait(block)

    def finish(self):
        @pl.loop(0, self.send.shape[1])
        def _(block):
            for peer in self.peers():
                self.copy(block, peer, self.me).wait_send()


def stages(blocks):
    lag = LAG
    first_shrink = blocks + lag
    second_shrink = first_shrink + blocks + 2 * lag
    return lag, first_shrink, second_shrink, second_shrink + blocks


def whole_kernel(
    levels_ref, steps_ref, to_high, to_low, back_high, back_low,
    left_hbm, right_hbm, recorded_ref, ranks_ref, scales_ref,
    out_ref,
    left, right, left_sem, right_sem, weight_left_ref, weight_right_ref,
    tile_send, tile_recv, freq_send, freq_recv, tile_ssem, tile_rsem, freq_ssem, freq_rsem,
    kept, wide, packed,
):
    step = pl.program_id(0)
    block = left.shape[1]
    rank = left.shape[5]
    blocks = tile_send.shape[2]
    lag, first_shrink, second_shrink, last = stages(blocks)
    tables = (to_high, to_low, back_high, back_low)
    over_tile = [
        Exchange("tile", tile_send.at[n], tile_recv.at[n], tile_ssem.at[n], tile_rsem.at[n])
        for n in range(tile_send.shape[0])
    ]
    over_freq = [
        Exchange("freq", freq_send.at[n], freq_recv.at[n], freq_ssem.at[n], freq_rsem.at[n])
        for n in range(freq_send.shape[0])
    ]

    all_rows = right.shape[2]

    def left_base(at):
        return at * block * all_rows + lax.axis_index("tile") * left.shape[2]

    def span(start):
        return (step >= start) & (step < start + blocks)

    def fetch(source, target, sem, at):
        return pltpu.make_async_copy(
            source.at[pl.ds(at * block, block)], target.at[at], sem.at[at]
        )

    def fetch_both(at):
        fetch(left_hbm, left, left_sem, at).start()
        fetch(right_hbm, right, right_sem, at).start()

    @pl.when(step == 0)
    def _():
        for at in range(min(AHEAD, blocks)):
            fetch_both(at)

    @pl.when(step + AHEAD < blocks)
    def _():
        fetch_both(step + AHEAD)

    @pl.when(step == 0)
    def _():
        barrier = pltpu.get_barrier_semaphore()
        count = 0
        for exchange in (over_tile[0], over_freq[0]):
            for peer in exchange.peers():
                pl.semaphore_signal(
                    barrier, inc=1, device_id={exchange.axis: peer},
                    device_id_type=pl.DeviceIdType.MESH,
                )
                count += 1
        lane_weights(ranks_ref, scales_ref, 0, weight_left_ref, rank)
        first_tile = lax.axis_index("tile") * right.shape[3]
        lane_weights(ranks_ref, scales_ref, first_tile, weight_right_ref, rank)
        pl.semaphore_wait(barrier, count)

    @pl.when(span(0))
    def _():
        fetch(left_hbm, left, left_sem, step).wait()
        dual_kernel(
            left_base(step), all_rows, left.at[step], recorded_ref, weight_left_ref,
            over_tile[0].send.at[:, step],
        )
        over_tile[0].start(step)

    def spread(start, tiles, freqs):
        @pl.when(span(start))
        def _():
            b = step - start
            if start == lag:
                fetch(right_hbm, right, right_sem, b).wait()
            tiles.wait(b)
            spread_kernel(
                b * block, steps_ref, right.at[b], tiles.recv.at[:, b], freqs.send.at[:, b]
            )
            freqs.start(b)

    spread(lag, over_tile[0], over_freq[0])

    @pl.when(step == first_shrink)
    def _():
        over_freq[0].wait_all()
        shrink_kernel(
            False, levels_ref, tables, over_freq[0].recv, kept, over_freq[1].send, wide, packed
        )
        over_freq[1].start_all()

    @pl.when(span(first_shrink))
    def _():
        b = step - first_shrink
        over_freq[1].wait(b)
        project_kernel(
            b * block, right.at[b], over_freq[1].recv.at[:, b], weight_right_ref,
            over_tile[1].send.at[:, b],
        )
        over_tile[1].start(b)

    @pl.when(span(first_shrink + lag))
    def _():
        b = step - first_shrink - lag
        over_tile[1].wait(b)
        image_kernel(
            left_base(b), all_rows, left.at[b], over_tile[1].recv.at[:, b], recorded_ref, weight_left_ref,
            over_tile[2].send.at[:, b],
        )
        over_tile[2].start(b)

    spread(first_shrink + 2 * lag, over_tile[2], over_freq[2])

    @pl.when(step == second_shrink)
    def _():
        over_freq[2].wait_all()
        shrink_kernel(
            True, levels_ref, tables, over_freq[2].recv, kept, over_freq[3].send, wide, packed
        )
        over_freq[3].start_all()

    @pl.when(span(second_shrink))
    def _():
        b = step - second_shrink
        over_freq[3].wait(b)
        peers, _, at_once, rows, width = over_freq[3].recv.shape
        for at in range(at_once):
            for peer in range(peers):
                out_ref[at, :, peer * width : (peer + 1) * width] = over_freq[3].recv[
                    peer, b, at
                ]

    @pl.when(step == last - 1)
    def _():
        for exchange in over_tile + over_freq:
            exchange.finish()


LAG = 2
AHEAD = 3


def lane_weights(ranks_ref, scales_ref, first_tile, out_ref, rank):
    freqs, rows, tiles = ranks_ref.shape
    lanes = out_ref.shape[1]
    owner = first_tile + lax.broadcasted_iota(jnp.int32, (tiles, lanes), 1) // (2 * rank)
    pick = (owner == lax.broadcasted_iota(jnp.int32, (tiles, lanes), 0)).astype(jnp.float32)
    widen = lambda values: jnp.dot(
        values.reshape(freqs * rows, tiles), pick, precision=lax.Precision.HIGHEST,
        preferred_element_type=jnp.float32,
    )
    slot = (lane_ids(freqs * rows, lanes) % rank).astype(jnp.float32)
    ranks = widen(ranks_ref[...].astype(jnp.float32))
    scales = widen(scales_ref[:, 0] * scales_ref[:, 1])
    out_ref[...] = jnp.where(slot < ranks - 0.5, scales, 0.0)


def table_parts():
    times = 2 * F
    freq = np.arange(F)[:, None]
    angles = (freq * np.arange(times)[None, :] % times) * (2.0 * math.pi / times)
    scaling = np.where(freq == 0, math.sqrt(1.0 / times), math.sqrt(2.0 / times))
    table = np.stack([scaling * np.cos(angles), -scaling * np.sin(angles)], 1)
    table = table.reshape(2 * F, times).astype(np.float32)
    high = table.astype(jnp.bfloat16)
    low = (table - high.astype(np.float32)).astype(jnp.bfloat16)
    return tuple(jnp.asarray(part) for part in (high.T, low.T, high, low))


def vmem():
    return pl.BlockSpec(memory_space=pltpu.VMEM)


def smem():
    return pl.BlockSpec(memory_space=pltpu.SMEM)


def per_device(
    left_factor, right_factor, tile_ranks, tile_scales, recorded, step_sizes, thresholds
):
    freqs, rows_here, col_tiles, _, rank, width = left_factor.shape
    row_tiles, cols_here = right_factor.shape[1:3]
    virtual = recorded.shape[2]
    tile_size = col_tiles // cols_here
    share = cols_here * 2 * rank
    lines = rows_here * virtual
    block = 2 if freqs % 2 == 0 else 1
    blocks = freqs // block
    lag, first_shrink, second_shrink, steps = stages(blocks)

    def spec(array, index):
        rest = array.shape[1:]
        return pl.BlockSpec((block,) + rest, lambda s: (index(s),) + (0,) * len(rest))

    def within(at):
        return jnp.minimum(jnp.maximum(at, 0), blocks - 1)

    def left_index(s):
        return jnp.where(s < blocks, s, within(s - first_shrink - lag))

    def out_index(s):
        return within(s - second_shrink)

    out_shape = (freqs, 2 * virtual, cols_here * width)
    dma = pltpu.SemaphoreType.DMA
    tile_buffer = pltpu.VMEM((3, tile_size, blocks, block, lines, share), jnp.bfloat16)
    freq_buffer = pltpu.VMEM((4, cols_here, blocks, block, 2 * virtual, width), jnp.bfloat16)
    wide = pltpu.VMEM((width // 128, 2 * F * virtual, 128), jnp.float32)
    estimate = pl.pallas_call(
        whole_kernel,
        out_shape=jax.ShapeDtypeStruct(out_shape, jnp.bfloat16),
        grid=(steps,),
        in_specs=[smem(), smem()]
        + [vmem()] * 4
        + [pl.BlockSpec(memory_space=pl.ANY)] * 2
        + [spec(recorded, left_index), vmem(), vmem()],
        out_specs=pl.BlockSpec((block,) + out_shape[1:], lambda s: (out_index(s), 0, 0)),
        scratch_shapes=[
            pltpu.VMEM((blocks, block) + left_factor.shape[1:], jnp.bfloat16),
            pltpu.VMEM((blocks, block) + right_factor.shape[1:], jnp.bfloat16),
            dma((blocks,)),
            dma((blocks,)),
            pltpu.VMEM((freqs * row_tiles, col_tiles * 2 * rank), jnp.float32),
            pltpu.VMEM((freqs * row_tiles, share), jnp.float32),
            tile_buffer,
            tile_buffer,
            freq_buffer,
            freq_buffer,
            dma((3, blocks, tile_size)),
            dma((3, blocks, tile_size)),
            dma((4, blocks, cols_here)),
            dma((4, blocks, cols_here)),
            pltpu.VMEM((virtual, 2 * F, width), jnp.float32),
            wide,
            wide,
        ],
        compiler_params=pltpu.CompilerParams(
            vmem_limit_bytes=58 << 20,
            dimension_semantics=("arbitrary",),
            collective_id=0,
            has_side_effects=True,
        ),
    )(
        thresholds, step_sizes, *table_parts(), left_factor, right_factor, recorded,
        tile_ranks, tile_scales,
    )
    return estimate.astype(jnp.float32).reshape(freqs, 2, virtual, cols_here * width)


def either(*arrays):
    left_factor, right_factor = arrays[:2]
    cols_here = right_factor.shape[2]
    rank, width = left_factor.shape[4:]
    aligned = (
        cols_here == lax.axis_size("freq")
        and width % 128 == 0
        and 128 % (2 * rank) == 0
        and (cols_here * 2 * rank) % 128 == 0
        and arrays[4].shape[2] == 8
        and right_factor.shape[1] % 8 == 0
        and left_factor.shape[0] * lax.axis_size("freq") == F
    )
    return (per_device if aligned else per_device_plain)(*arrays)


def solution(mesh):
    return jax.shard_map(
        either,
        mesh=mesh,
        in_specs=(
            P("freq", "tile", None, None, None, None),
            P("freq", None, "tile", None, None, None),
            P("freq", None, None),
            P("freq", None, None, None),
            P("freq", None, None, "tile"),
            P("freq"),
            P(),
        ),
        out_specs=P("freq", None, None, "tile"),
        check_vma=False,
    )
```
